256 devices in a mesh: ctx: 8 (over x, y_hi), mp: 32 (over z, y_lo, core).
Axes of the slice: x: 4, y: 4 (y_hi: 2, y_lo: 2; y = y_hi * 2 + y_lo), z: 8, core: 2. Of those that a mesh axis runs over, the one named last changes fastest.
Arguments:
- activations: bfloat16 [8192, 4096], P('ctx', 'mp'), may hold values from -36 to 36
- norm_gain: float32 [4096], P('mp'), may hold values from 0.1 to 1.9
- w_in: bfloat16 [4096, 3, 4096], P('ctx', None, 'mp'), may hold values from -0.09375 to 0.09375
- tail_rows: bfloat16 [3, 4096, 2], P(None, 'mp'), may hold values from -4 to 4
- short_filter: float32 [3, 3, 4096], P(None, None, 'mp'), may hold values from -3 to 3
- decay_rate: float32 [4096, 16], P('mp'), may hold values from 2.4414063e-05 to 0.08, as said below
- residue: float32 [4096, 16], P('mp'), may hold values from -1.5 to 1.5
- skip_gain: float32 [4096], P('mp'), may hold values from -4 to 4
- state_in: float32 [4096, 16], P('mp'), may hold values from -4 to 4
- w_out: bfloat16 [4096, 4096], P('mp', 'ctx'), may hold values from -0.1875 to 0.1875
Outputs:
- block_out: bfloat16 [8192, 4096], P('ctx', 'mp')
- state_out: float32 [4096, 16], P('mp')
The draws below stay inside these ranges and needn't reach their ends.
Inputs may be any that keep to these rules, and one draw needn't show every extreme that they name: `decay_rate`: every rate lies between 0.2/8192 and 0.08; any share of the modes may be slow (below 2/8192) or fast.
All inputs are finite; a program needn't handle non-finite values.
Results may differ from the reference program's by a relative error of at most 0.03.
Values may be sent and summed in bfloat16 or wider, within the bound.
A program may use at most 64 MiB of HBM per device.

```python
import math
import jax
import jax.numpy as jnp
from jax import lax

D = 4096
ORDER = 16
TOKENS = 8192


def draw_activations(key, part):
    row_scale = jnp.exp(jax.random.uniform(jax.random.fold_in(key, 11), (TOKENS, 1), jnp.float32, math.log(0.3), math.log(3.0)))
    col_scale = jnp.exp(jax.random.uniform(jax.random.fold_in(key, 12), (1, D), jnp.float32, math.log(0.3), math.log(3.0)))
    base = jnp.clip(jax.random.normal(jax.random.fold_in(key, 15), (TOKENS, D), jnp.float32), -4.0, 4.0)
    return (base * row_scale * col_scale).astype(jnp.bfloat16)


def draw_decay_rate(key, part):
    lowest = 0.2 / TOKENS
    border = 2.0 / TOKENS
    highest_rate = 0.08
    chooser = jax.random.uniform(jax.random.fold_in(key, 21), (D, ORDER), jnp.float32)
    slow_rate = jnp.exp(jax.random.uniform(jax.random.fold_in(key, 22), (D, ORDER), jnp.float32, math.log(lowest), math.log(border)))
    fast_rate = jnp.exp(jax.random.uniform(jax.random.fold_in(key, 23), (D, ORDER), jnp.float32, math.log(border), math.log(highest_rate)))
    result = jnp.where(chooser < 0.5, slow_rate, fast_rate)
    return result.astype(jnp.float32)


def strengthened(values, own_key, source, target, blocks, factor):
    def block_of(axis_at):
        return (jnp.arange(values.shape[axis_at]) // (values.shape[axis_at] // blocks)).reshape((-1,) + (1,) * (values.ndim - 1 - axis_at))

    one_side = jax.random.permutation(own_key, blocks)[block_of(target)]
    other_side = (block_of(target) + blocks // 2) % blocks
    return jnp.where((block_of(source) == one_side) | (block_of(source) == other_side), factor * values, values)


def level_of(stream_key, dims, cuts, least, high):
    def one(axis_at, parts):
        heights = jax.random.uniform(jax.random.fold_in(jax.random.fold_in(stream_key, 6), axis_at), (parts,), jnp.float32, least / len(cuts), high / len(cuts))
        return jnp.repeat(jnp.exp(heights), dims[axis_at] // parts).reshape((-1,) + (1,) * (len(dims) - axis_at - 1))

    level = one(*cuts[0])
    for cut in cuts[1:]:
        level = level * one(*cut)
    return level


def scatter_about(own_key, dims, deviation, reach, split=(), held_as=jnp.bfloat16):
    values = jax.random.normal(own_key, dims, jnp.float32) * deviation
    if len(split) > 0:
        values = level_of(own_key, dims, split, -0.22, 0.18) * values
    return jnp.clip(values, min=-reach, max=reach).astype(held_as)


def noise_with(key, extent, deviation, most, cuts, heavy, kind=jnp.bfloat16):
    drawn = deviation * jax.random.normal(key, extent, jnp.float32)
    if cuts:
        drawn = drawn * level_of(key, extent, cuts, -0.22, 0.18)
    return jnp.clip(strengthened(drawn, jax.random.fold_in(key, 3), *heavy), -most, most).astype(kind)


def setup_inputs(seed: int = 0) -> dict:
    arg_keys = jax.random.split(jax.random.key(seed), 11)
    return {
        "activations": draw_activations(jax.random.fold_in(arg_keys[10], 71), 0),
        "norm_gain": jnp.clip(1.0 + 0.18 * jax.random.normal(arg_keys[1], (D,), jnp.float32), 0.1, 1.9),
        "w_in": scatter_about(arg_keys[2], (D, 3, D), D ** -0.5, 0.09375, ((0, 8), (2, 32))),
        "tail_rows": scatter_about(arg_keys[3], (3, D, 2), 1.0, 4.0, ((1, 32),)),
        "short_filter": scatter_about(arg_keys[4], (3, 3, D), 0.6, 3.0, ((2, 32),), jnp.float32),
        "decay_rate": draw_decay_rate(jax.random.fold_in(arg_keys[10], 71), 0),
        "residue": scatter_about(arg_keys[6], (D, ORDER), 0.25, 1.5, ((0, 32),), jnp.float32),
        "skip_gain": scatter_about(arg_keys[7], (D,), 1.0, 4.0, ((0, 32),), jnp.float32),
        "state_in": scatter_about(arg_keys[8], (D, ORDER), 1.0, 4.0, ((0, 32),), jnp.float32),
        "w_out": noise_with(arg_keys[9], (D, D), D ** -0.5, 0.1875, ((0, 32), (1, 8)), (0, 1, 32, 2.75)),
    }


def reference(activations, norm_gain, w_in, tail_rows, short_filter, decay_rate, residue, skip_gain, state_in, w_out):
    act_float = activations.astype(jnp.float32)
    inverse = lax.rsqrt(lax.optimization_barrier(jnp.mean(act_float * act_float, axis=1, keepdims=True)) + 1e-06)
    normed = (act_float * inverse * norm_gain[None, :]).astype(jnp.bfloat16)
    model_width = activations.shape[1]
    flat = jnp.dot(normed, w_in.reshape(model_width, 3 * model_width), preferred_element_type=jnp.float32)
    projected = flat.astype(jnp.bfloat16).reshape(-1, 3, model_width).transpose(1, 2, 0)
    extended = jnp.concatenate([tail_rows, projected], axis=2).astype(jnp.float32)
    smoothed = short_filter[0][:, :, None] * extended[:, :, 2:]
    smoothed = smoothed + short_filter[1][:, :, None] * extended[:, :, 1:-1]
    smoothed = smoothed + short_filter[2][:, :, None] * extended[:, :, :-2]
    query = smoothed[0]
    mixed = (smoothed[1] * smoothed[2]).astype(jnp.bfloat16)
    mixed_float = mixed.astype(jnp.float32)
    decays = jnp.exp(-decay_rate)
    scales = jnp.sqrt(-jnp.expm1(-2.0 * decay_rate))

    def advance(state, column):
        state = decays * state + scales * column[:, None]
        return (state, lax.optimization_barrier(jnp.sum(residue * state, axis=1)))
    state_out, outputs = lax.scan(advance, state_in, mixed_float.T)
    response = outputs.T + skip_gain[:, None] * mixed_float
    gated = (query * response).astype(jnp.bfloat16)
    branch = jnp.dot(gated.T, w_out, preferred_element_type=jnp.float32)
    return ((act_float + branch).astype(jnp.bfloat16), state_out)
```

```python
import jax
import jax.numpy as jnp
from jax import lax
from jax.experimental import pallas as pl
from jax.experimental.pallas import tpu as pltpu
from jax.sharding import PartitionSpec as P

MESH = pl.DeviceIdType.MESH
F32, BF16 = jnp.float32, jnp.bfloat16

NI, NJ = 8, 32
NZ, NX = 8, 4
T, F, D, ORDER = 1024, 128, 4096, 16
H = T // 2
HG = H + 16
CH = 8
CL = T // CH
TILE = 256
N_SEND = 160
PLUS_HOPS = {"own0": 4, "own1": 3, "par1": 4}
MINUS_HOPS = {"own0": 3, "own1": 4, "par1": 3}


def one_minus_exp_neg(v):
    series = 1.0 - v * (1.0 / 8.0)
    for k in (7, 6, 5, 4, 3, 2):
        series = 1.0 - v * (1.0 / k) * series
    return v * series


def block_kernel(
    act, gain, w_local, tail, filt, rate, resid, skip, st_in, wout,
    out, st_out,
    xg, wg, ext, ssq, mx, ts, endb, ends, gf, gg, ws, wo, acc, osend, orecv,
    ssem, xr, wr, hr, er, wor, gr, orr,
):
    i, j = lax.axis_index("ctx"), lax.axis_index("mp")
    z, yl, c = j // 4, (j // 2) % 2, j % 2
    at = lambda zz, yy, cc: zz * 4 + yy * 2 + cc
    up, down = (z + 1) % NZ, (z + NZ - 1) % NZ
    dev_up, dev_down = (i, at(up, yl, c)), (i, at(down, yl, c))
    dev_y, dev_c = (i, at(z, 1 - yl, c)), (i, at(z, yl, 1 - c))
    ix_up, ix_down = (i + 2) % NI, (i + NI - 2) % NI
    pair = i + 1 - 2 * (i % 2)
    dev_xu, dev_xd, dev_yh = (ix_up, j), (ix_down, j), (pair, j)

    sends = []

    def send(src, dst, recv_sem, dev):
        copy = pltpu.make_async_remote_copy(
            src_ref=src, dst_ref=dst, send_sem=ssem.at[len(sends)], recv_sem=recv_sem,
            device_id=dev, device_id_type=MESH,
        )
        sends.append((copy, None))
        copy.start()

    def send_if(cond, src, dst, recv_sem, dev):
        copy = pltpu.make_async_remote_copy(
            src_ref=src, dst_ref=dst, send_sem=ssem.at[len(sends)], recv_sem=recv_sem,
            device_id=dev, device_id_type=MESH,
        )
        sends.append((copy, cond))
        pl.when(cond)(lambda: copy.start())

    def arrived(dst, recv_sem):
        pltpu.make_async_remote_copy(
            src_ref=dst, dst_ref=dst, send_sem=ssem.at[0], recv_sem=recv_sem,
            device_id=dev_up, device_id_type=MESH,
        ).wait_recv()

    barrier = pltpu.get_barrier_semaphore()

    def tell(dev):
        pl.semaphore_signal(barrier, inc=1, device_id=dev, device_id_type=MESH)

    for dev in (dev_up, dev_down, dev_y, dev_c):
        tell(dev)
    for k in range(1, NI):
        tell(((i + k) % NI, j))
    self_out = z == i
    for k in range(16):
        zz, cc = (z + k // 2) % NZ, (c + k % 2) % 2
        if k == 0:
            pl.when(jnp.logical_not(self_out))(lambda: tell((z, at(z, yl, c))))
        else:
            tell((z, at(zz, yl, cc)))

    g = gain[...]
    g_hi = g.astype(BF16)
    g_rest = g - g_hi.astype(F32)
    g_mid = g_rest.astype(BF16)
    g_lo = (g_rest - g_mid.astype(F32)).astype(BF16)
    row16 = lax.broadcasted_iota(jnp.int32, (16, F), 0)
    zero16 = jnp.zeros((16, F), F32)
    g_rows = jnp.where(
        row16 == 0, g_hi.astype(F32) + zero16,
        jnp.where(row16 == 1, g_mid.astype(F32) + zero16,
                  jnp.where(row16 == 2, g_lo.astype(F32) + zero16, zero16)),
    ).astype(BF16)
    for h in range(2):
        xg[h, j, 0:H, :] = act[h * H:(h + 1) * H, :]
        xg[h, j, H:HG, :] = g_rows
    wg[i, 0] = w_local[0:256, :]
    wg[i, 1] = w_local[256:512, :]
    for c2 in range(2):
        lo, hi = wout[:, c2 * F:(c2 + 1) * F], wout[:, (2 + c2) * F:(3 + c2) * F]
        ws[c2, 0] = jnp.where(yl == 0, lo, hi)
        ws[c2, 1] = jnp.where(yl == 0, hi, lo)

    peers = 4 + NI - 1 + 16
    pl.when(self_out)(lambda: pl.semaphore_wait(barrier, peers - 1))
    pl.when(jnp.logical_not(self_out))(lambda: pl.semaphore_wait(barrier, peers))

    def x_send(h, jj, dev):
        send(xg.at[h, jj], xg.at[h, jj], xr.at[h, jj], dev)

    def x_wait(h, jj):
        arrived(xg.at[h, jj], xr.at[h, jj])

    def w_send(ii, half, dev):
        send(wg.at[ii, half], wg.at[ii, half], wr.at[ii, half], dev)

    def w_wait(ii, half):
        arrived(wg.at[ii, half], wr.at[ii, half])

    for h in range(2):
        x_send(h, j, dev_y)
        x_send(h, j, dev_up)
        x_send(h, j, dev_down)
        x_send(h, j, dev_c)
    for half in range(2):
        w_send(i, half, dev_yh)
        w_send(i, half, dev_xu)
        w_send(i, half, dev_xd)

    def clear(r, carry):
        ext[:, pl.ds(8 + r * 128, 128), :] = jnp.zeros((3, 128, F), F32)
        ssq[pl.ds(r * 128, 128), :] = jnp.zeros((128, F), F32)
        return carry

    lax.fori_loop(0, T // 128, clear, 0)

    jp = at(z, 1 - yl, c)
    x_wait(1, jp)
    x_send(1, jp, dev_up)
    x_send(1, jp, dev_down)
    x_send(1, jp, dev_c)
    x_wait(0, jp)
    x_send(0, jp, dev_c)
    for half in range(2):
        w_wait(pair, half)
        w_send(pair, half, dev_xu)
        w_send(pair, half, dev_xd)

    def x_step(s):
        for plus in (True, False):
            zo = (z + NZ - s) % NZ if plus else (z + s) % NZ
            hops = PLUS_HOPS if plus else MINUS_HOPS
            dev = dev_up if plus else dev_down
            for name, h, yy in (("own0", 0, yl), ("own1", 1, yl), ("par1", 1, 1 - yl)):
                if s > hops[name]:
                    continue
                jj = at(zo, yy, c)
                x_wait(h, jj)
                if s < hops[name]:
                    x_send(h, jj, dev)
                if name == "own0":
                    x_send(h, jj, dev_y)
                x_send(h, jj, dev_c)

    def x_late(s):
        for zo in ((z + NZ - s) % NZ, (z + s) % NZ)[: 1 if s == NZ // 2 else 2]:
            jj = at(zo, 1 - yl, c)
            x_wait(0, jj)
            x_send(0, jj, dev_c)

    def x_other_core(s):
        for zo in ((z + NZ - s) % NZ, (z + s) % NZ)[: 1 if s in (0, NZ // 2) else 2]:
            for yy in range(2):
                for h in range(2):
                    x_wait(h, at(zo, yy, 1 - c))

    def multiply(zo, yy, r):
        h, rows = r // 2, pl.ds(pl.multiple_of((r % 2) * TILE, TILE), TILE)
        total = pl.ds(pl.multiple_of(r * TILE, TILE), TILE)
        parts, squares = [], None
        for cc in range(2):
            jj = at(zo, yy, cc)
            block = xg[h, jj, rows, :].astype(F32)
            gains = jnp.sum(xg[h, jj, pl.ds(H, 16), :].astype(F32), axis=0, keepdims=True)
            parts.append((block * gains).astype(BF16))
            squares = block * block if squares is None else squares + block * block
        ssq[total, :] += squares
        into = pl.ds(pl.multiple_of(8 + r * TILE, 8), TILE)
        product = jnp.dot(jnp.concatenate(parts, axis=1), wg[zo, yy], preferred_element_type=F32)
        for q in range(3):
            ext[q, into, :] += product[:, q * F:(q + 1) * F]

    def compute(s):
        blocks = 2 if s in (0, NZ // 2) else 4

        def body(k, carry):
            blk, r = k // 4, k % 4
            zo = (z + NZ - s + (blk // 2) * 2 * s) % NZ
            multiply(zo, blk % 2, r)
            return carry

        lax.fori_loop(0, blocks * 4, body, 0)

    x_step(1)
    for half in (0, 1):
        w_wait(ix_down, half)
        if half == 0:
            w_send(ix_down, 0, dev_xu)
        w_wait(ix_up, half)
        if half == 1:
            w_send(ix_up, 1, dev_xd)
    x_step(2)
    x_late(1)
    pd, pu = (pair + NI - 2) % NI, (pair + 2) % NI
    for half in (0, 1):
        w_wait(pd, half)
        if half == 0:
            w_send(pd, 0, dev_xu)
        w_wait(pu, half)
        if half == 1:
            w_send(pu, 1, dev_xd)
    x_step(3)
    x_late(2)
    far, pfar = (i + 4) % NI, (pair + 4) % NI
    for half in range(2):
        w_wait(far, half)
    for half in range(2):
        w_wait(pfar, half)
    x_other_core(0)
    compute(0)
    x_late(3)
    x_other_core(1)
    compute(1)
    x_step(4)

    slot = z * 2 + c
    for k in range(16):
        i2, c2 = (i + k // 2) % NI, (c + k % 2) % 2
        dev = (i2, at(i, yl, c2))
        if k == 0:
            send_if(jnp.logical_not(self_out), ws.at[c2], wo.at[slot], wor.at[slot], dev)
        else:
            send(ws.at[c2], wo.at[slot], wor.at[slot], dev)

    @pl.when(self_out)
    def _():
        wo[slot] = ws[c]

    x_late(4)
    x_other_core(2)
    compute(2)
    x_other_core(3)
    compute(3)
    x_other_core(4)
    compute(4)

    def normalise(r, carry):
        rows = pl.ds(pl.multiple_of(r * 128, 128), 128)
        into = pl.ds(pl.multiple_of(8 + r * 128, 8), 128)
        total = jnp.sum(ssq[rows, :], axis=1, keepdims=True)
        inverse = lax.rsqrt(total * (1.0 / D) + 1e-06)
        ext[:, into, :] = (ext[:, into, :] * inverse[None]).astype(BF16).astype(F32)
        return carry

    lax.fori_loop(0, T // 128, normalise, 0)
    send_if(i < NI - 1, ext.at[:, pl.ds(T, 8)], ext.at[:, pl.ds(0, 8)], hr, ((i + 1) % NI, j))

    rate_t, resid_t = rate[...].T, resid[...].T
    scale_t = jnp.sqrt(one_minus_exp_neg(2.0 * rate_t))
    weight_t = resid_t * scale_t
    lam_t = jnp.exp(-rate_t)

    def wide(table, n):
        return jnp.broadcast_to(table[n:n + 1, :], (CH, F))

    lam = [wide(lam_t, n) for n in range(ORDER)]
    tap = lambda t, q: jnp.broadcast_to(filt[t, q:q + 1, :], (CH, F))

    @pl.when(i == 0)
    def _():
        ext[:, 0:8, :] = tail[...]

    @pl.when(i > 0)
    def _():
        arrived(ext.at[:, pl.ds(0, 8)], hr)

    def chunk_rows(start, q):
        return ext[q, pl.ds(start, CH, stride=CL), :]

    kt, vt = [tap(t, 1) for t in range(3)], [tap(t, 2) for t in range(3)]
    U = 4

    def first(it, carry):
        k1, k2, v1, v2 = carry[:4]
        state = list(carry[4:])
        for u in range(U):
            s = it * U + u
            k0, v0 = chunk_rows(8 + s, 1), chunk_rows(8 + s, 2)
            keys = kt[0] * k0 + kt[1] * k1 + kt[2] * k2
            values = vt[0] * v0 + vt[1] * v1 + vt[2] * v2
            m = (keys * values).astype(BF16).astype(F32)
            mx[s] = m
            state = [lam[n] * state[n] + m for n in range(ORDER)]
            k1, k2, v1, v2 = k0, k1, v0, v1
        return (k1, k2, v1, v2, *state)

    zero = jnp.zeros((CH, F), F32)
    carry = lax.fori_loop(
        0, CL // U, first,
        (chunk_rows(7, 1), chunk_rows(6, 1), chunk_rows(7, 2), chunk_rows(6, 2)) + (zero,) * ORDER,
    )
    row8 = lax.broadcasted_iota(jnp.int32, (CH, F), 0)
    for n in range(ORDER):
        total, r = carry[4 + n], jnp.broadcast_to(rate_t[n:n + 1, :], (CH, F))
        for shift in (1, 2, 4):
            moved = jnp.where(row8 >= shift, pltpu.roll(total, shift, axis=0), 0.0)
            total = total + jnp.exp(-r * float(CL * shift)) * moved
        ts[n] = total
        endb[n:n + 1, :] = total[CH - 1:CH, :]
    ends[i] = endb[...]
    for k in range(1, NI):
        send(endb, ends.at[i], er.at[i], ((i + k) % NI, j))
    start_t = st_in[...].T / scale_t
    whole = jnp.exp(-rate_t * float(T))
    for k in range(1, NI):
        arrived(ends.at[(i + k) % NI], er.at[(i + k) % NI])
    now, mine = start_t, start_t
    for k in range(NI):
        mine = jnp.where(i == k, now, mine)
        now = whole * now + ends[k]
    st_out[...] = (now * scale_t).T

    qt = [tap(t, 0) for t in range(3)]
    weight = [wide(weight_t, n) for n in range(ORDER)]
    direct = jnp.broadcast_to(skip[...], (CH, F))
    chunk_start = row8.astype(F32) * float(CL)
    entering = []
    for n in range(ORDER):
        r = jnp.broadcast_to(rate_t[n:n + 1, :], (CH, F))
        before = jnp.where(row8 >= 1, pltpu.roll(ts[n], 1, axis=0), 0.0)
        entering.append(before + jnp.exp(-r * chunk_start) * jnp.broadcast_to(mine[n:n + 1, :], (CH, F)))

    def second(it, carry):
        q1, q2 = carry[:2]
        state = list(carry[2:])
        for u in range(U):
            s = it * U + u
            q0 = chunk_rows(8 + s, 0)
            query = qt[0] * q0 + qt[1] * q1 + qt[2] * q2
            m = mx[s]
            state = [lam[n] * state[n] + m for n in range(ORDER)]
            terms = [weight[n] * state[n] for n in range(ORDER)] + [direct * m]
            while len(terms) > 1:
                terms = [a + b for a, b in zip(terms[::2], terms[1::2])] + terms[len(terms) & ~1:]
            gf[pl.ds(s, CH, stride=CL), :] = query * terms[0]
            q1, q2 = q0, q1
        return (q1, q2, *state)

    lax.fori_loop(0, CL // U, second, (chunk_rows(7, 0), chunk_rows(6, 0), *entering))

    own = z * 2 + c
    for h in range(2):
        gg[h, own] = gf[h * H:(h + 1) * H, :].astype(BF16)

    def g_send(h, ss, dev):
        send(gg.at[h, ss], gg.at[h, ss], gr.at[h, ss], dev)

    def g_wait(h, ss):
        arrived(gg.at[h, ss], gr.at[h, ss])

    for h in range(2):
        g_send(h, own, dev_up)
        g_send(h, own, dev_down)
        g_send(h, own, dev_c)

    pl.when(jnp.logical_not(self_out))(lambda: arrived(wo.at[slot], wor.at[slot]))
    for k in range(1, 16):
        src = ((z + k // 2) % NZ) * 2 + (c + k % 2) % 2
        arrived(wo.at[src], wor.at[src])

    def clear_acc(r, carry):
        acc[pl.ds(r * 128, 128), :] = jnp.zeros((128, 2 * F), F32)
        return carry

    lax.fori_loop(0, T // 128, clear_acc, 0)

    def g_step(s):
        for plus in (True, False):
            zo = (z + NZ - s) % NZ if plus else (z + s) % NZ
            dev = dev_up if plus else dev_down
            for h in range(2):
                hops = 4 if plus == (h == 0) else 3
                if s > hops:
                    continue
                g_wait(h, zo * 2 + c)
                if s < hops:
                    g_send(h, zo * 2 + c, dev)
                g_send(h, zo * 2 + c, dev_c)

    def g_compute(s):
        origins = ((z + NZ - s) % NZ, (z + s) % NZ)[: 1 if s in (0, NZ // 2) else 2]
        for zo in origins:
            for h in range(2):
                g_wait(h, zo * 2 + 1 - c)

        def body(k, carry):
            zo = (z + NZ - s + (k // 4) * 2 * s) % NZ
            r = k % 4
            h, rows = r // 2, pl.ds(pl.multiple_of((r % 2) * TILE, TILE), TILE)
            total = pl.ds(pl.multiple_of(r * TILE, TILE), TILE)
            left = jnp.concatenate([gg[h, zo * 2, rows, :], gg[h, zo * 2 + 1, rows, :]], axis=1)
            right = jnp.concatenate(
                [jnp.concatenate([wo[zo * 2 + cc, 0], wo[zo * 2 + cc, 1]], axis=1) for cc in range(2)], axis=0
            )
            acc[total, :] += jnp.dot(left, right, preferred_element_type=F32)
            return carry

        lax.fori_loop(0, 4 * len(origins), body, 0)

    g_step(1)
    g_compute(0)
    g_step(2)
    g_compute(1)
    g_step(3)
    g_compute(2)
    g_step(4)
    g_compute(3)
    g_compute(4)

    for h in range(2):
        osend[h] = acc[h * H:(h + 1) * H, F:2 * F].astype(BF16)
        send(osend.at[h], orecv.at[h], orr.at[h], dev_y)
    for h in range(2):
        arrived(orecv.at[h], orr.at[h])
        rows = slice(h * H, (h + 1) * H)
        out[rows, :] = (act[rows, :].astype(F32) + (acc[rows, 0:F] + orecv[h].astype(F32))).astype(BF16)

    for copy, cond in sends:
        if cond is None:
            copy.wait_send()
        else:
            pl.when(cond)(lambda copy=copy: copy.wait_send())


def local(activations, norm_gain, w_in, tail_rows, short_filter, decay_rate, residue, skip_gain, state_in, w_out):
    tail = jnp.pad(tail_rows.transpose(0, 2, 1).astype(F32), ((0, 0), (6, 0), (0, 0)))
    vmem = pl.BlockSpec(memory_space=pltpu.VMEM)
    dma = pltpu.SemaphoreType.DMA
    return pl.pallas_call(
        block_kernel,
        out_shape=(jax.ShapeDtypeStruct((T, F), BF16), jax.ShapeDtypeStruct((F, ORDER), F32)),
        in_specs=[vmem] * 10,
        out_specs=(vmem, vmem),
        scratch_shapes=[
            pltpu.VMEM((2, NJ, HG, F), BF16),
            pltpu.VMEM((NI, 2, 256, 3 * F), BF16),
            pltpu.VMEM((3, T + 8, F), F32),
            pltpu.VMEM((T, F), F32),
            pltpu.VMEM((CL, CH, F), F32),
            pltpu.VMEM((ORDER, CH, F), F32),
            pltpu.VMEM((ORDER, F), F32),
            pltpu.VMEM((NI, ORDER, F), F32),
            pltpu.VMEM((T, F), F32),
            pltpu.VMEM((2, 16, H, F), BF16),
            pltpu.VMEM((2, 2, F, F), BF16),
            pltpu.VMEM((16, 2, F, F), BF16),
            pltpu.VMEM((T, 2 * F), F32),
            pltpu.VMEM((2, H, F), BF16),
            pltpu.VMEM((2, H, F), BF16),
            dma((N_SEND,)),
            dma((2, NJ)),
            dma((NI, 2)),
            dma,
            dma((NI,)),
            dma((16,)),
            dma((2, 16)),
            dma((2,)),
        ],
        compiler_params=pltpu.CompilerParams(
            collective_id=0, has_side_effects=True, vmem_limit_bytes=56 << 20
        ),
    )(
        activations, norm_gain.reshape(1, F), w_in.reshape(512, 3 * F), tail, short_filter,
        decay_rate, residue, skip_gain.reshape(1, F), state_in, w_out,
    )


def solution(mesh):
    placed = (
        P("ctx", "mp"),
        P("mp"),
        P("ctx", None, "mp"),
        P(None, "mp", None),
        P(None, None, "mp"),
        P("mp", None),
        P("mp", None),
        P("mp"),
        P("mp", None),
        P("mp", "ctx"),
    )
    return jax.shard_map(
        local, mesh=mesh, in_specs=placed, out_specs=(P("ctx", "mp"), P("mp", None)), check_vma=False
    )
```

```python
import jax
import jax.numpy as jnp
from jax import lax
from jax.experimental import pallas as pl
from jax.experimental.pallas import tpu as pltpu
from jax.sharding import PartitionSpec as P

MESH = pl.DeviceIdType.MESH
F32, BF16 = jnp.float32, jnp.bfloat16

NI, NJ = 8, 32
NZ, NX = 8, 4
T, F, D, ORDER = 1024, 128, 4096, 16
H = T // 2
HG = H + 16
CH = 8
CL = T // CH
N_SEND = 176
PLUS_HOPS = {"own0": 4, "own1": 3, "par1": 4}
MINUS_HOPS = {"own0": 3, "own1": 4, "par1": 4}


def one_minus_exp_neg(v):
    series = 1.0 - v * (1.0 / 8.0)
    for k in (7, 6, 5, 4, 3, 2):
        series = 1.0 - v * (1.0 / k) * series
    return v * series


def block_kernel(
    act, gain, w_local, tail, filt, rate, resid, skip, st_in, wout,
    out, st_out,
    xg, xs, wg, wt, ext, ssq, mx, ts, endb, ends, gf, gk, ws, wo, pa, sb, rb,
    ssem, xr, wr, wtr, hr, er, wor, gr, rr,
):
    i, j = lax.axis_index("ctx"), lax.axis_index("mp")
    z, yl, c = j // 4, (j // 2) % 2, j % 2
    at = lambda zz, yy, cc: zz * 4 + yy * 2 + cc
    up, down = (z + 1) % NZ, (z + NZ - 1) % NZ
    dev_up, dev_down = (i, at(up, yl, c)), (i, at(down, yl, c))
    dev_y, dev_c = (i, at(z, 1 - yl, c)), (i, at(z, yl, 1 - c))
    ix_up, ix_down = (i + 2) % NI, (i + NI - 2) % NI
    pair = i + 1 - 2 * (i % 2)
    dev_xu, dev_xd, dev_yh = (ix_up, j), (ix_down, j), (pair, j)
    y = (i % 2) * 2 + yl
    yu, yd = (y + 1) % 4, (y + 3) % 4
    i_yu, i_yd = (i // 2) * 2 + yu // 2, (i // 2) * 2 + yd // 2
    dev_yu, dev_yd = (i_yu, at(z, yu % 2, c)), (i_yd, at(z, yd % 2, c))
    dev_yc = (i, at(z, 1 - yl, 1 - c))

    sends = []

    def send(src, dst, recv_sem, dev):
        copy = pltpu.make_async_remote_copy(
            src_ref=src, dst_ref=dst, send_sem=ssem.at[len(sends)], recv_sem=recv_sem,
            device_id=dev, device_id_type=MESH,
        )
        sends.append((copy, None))
        copy.start()

    def send_if(cond, src, dst, recv_sem, dev):
        copy = pltpu.make_async_remote_copy(
            src_ref=src, dst_ref=dst, send_sem=ssem.at[len(sends)], recv_sem=recv_sem,
            device_id=dev, device_id_type=MESH,
        )
        sends.append((copy, cond))
        pl.when(cond)(lambda: copy.start())

    def arrived(dst, recv_sem):
        pltpu.make_async_remote_copy(
            src_ref=dst, dst_ref=dst, send_sem=ssem.at[0], recv_sem=recv_sem,
            device_id=dev_up, device_id_type=MESH,
        ).wait_recv()

    barrier = pltpu.get_barrier_semaphore()

    def tell(dev):
        pl.semaphore_signal(barrier, inc=1, device_id=dev, device_id_type=MESH)

    for dev in (dev_up, dev_down, dev_c, dev_yu, dev_yd, dev_yc):
        tell(dev)
    for k in range(1, NI):
        tell(((i + k) % NI, j))

    g = gain[...]
    g_hi = g.astype(BF16)
    g_rest = g - g_hi.astype(F32)
    g_mid = g_rest.astype(BF16)
    g_lo = (g_rest - g_mid.astype(F32)).astype(BF16)
    row16 = lax.broadcasted_iota(jnp.int32, (16, F), 0)
    zero16 = jnp.zeros((16, F), F32)
    g_rows = jnp.where(
        row16 == 0, g_hi.astype(F32) + zero16,
        jnp.where(row16 == 1, g_mid.astype(F32) + zero16,
                  jnp.where(row16 == 2, g_lo.astype(F32) + zero16, zero16)),
    ).astype(BF16)
    for h in range(2):
        xg[h, j, 0:H, :] = act[h * H:(h + 1) * H, :]
        xg[h, j, H:HG, :] = g_rows
    for half in range(2):
        wg[i, half] = w_local[:, half * 256:(half + 1) * 256, :]
    for k in range(4):
        ws[k] = wout[:, k * F:(k + 1) * F]
    wo[i, yl, pl.ds(pl.multiple_of(c * F, F), F), :] = ws[yl * 2 + c]

    pl.semaphore_wait(barrier, 6 + NI - 1)

    def x_send(h, jj, dev):
        send(xg.at[h, jj], xg.at[h, jj], xr.at[h, jj], dev)

    def x_wait(h, jj):
        arrived(xg.at[h, jj], xr.at[h, jj])

    def w_send(ii, half, dev):
        send(wg.at[ii, half], wg.at[ii, half], wr.at[ii, half], dev)

    def w_wait(ii, half):
        arrived(wg.at[ii, half], wr.at[ii, half])

    for h in range(2):
        x_send(h, j, dev_y)
        x_send(h, j, dev_up)
        x_send(h, j, dev_down)
        x_send(h, j, dev_c)
    send(wg.at[i, 0], wt.at[0], wtr.at[0], dev_yu)
    send(wg.at[i, 1], wt.at[1], wtr.at[1], dev_yd)
    for half in range(2):
        w_send(i, half, dev_xu)
        w_send(i, half, dev_xd)

    mine_rows = pl.ds(pl.multiple_of(c * F, F), F)
    for dev, block in ((dev_c, yl * 2 + 1 - c), (dev_y, (1 - yl) * 2 + c), (dev_yc, (1 - yl) * 2 + 1 - c)):
        send(ws.at[block], wo.at[i, yl, mine_rows, :], wor.at[i, yl, c], dev)

    def clear(r, carry):
        ext[:, pl.ds(8 + r * 128, 128), :] = jnp.zeros((3, 128, F), F32)
        ssq[pl.ds(r * 128, 128), :] = jnp.zeros((128, F), F32)
        return carry

    lax.fori_loop(0, T // 128, clear, 0)

    jp = at(z, 1 - yl, c)
    x_wait(1, jp)
    x_send(1, jp, dev_up)
    x_send(1, jp, dev_down)
    x_send(1, jp, dev_c)
    x_wait(0, jp)
    x_send(0, jp, dev_c)
    arrived(wt.at[0], wtr.at[0])
    send(wt.at[0], wg.at[i_yd, 0], wr.at[i_yd, 0], dev_yu)
    arrived(wt.at[1], wtr.at[1])
    send(wt.at[1], wg.at[i_yu, 1], wr.at[i_yu, 1], dev_yd)
    for half in range(2):
        w_wait(pair, half)
        w_send(pair, half, dev_xu)
        w_send(pair, half, dev_xd)

    def x_step(s):
        for plus in (True, False):
            zo = (z + NZ - s) % NZ if plus else (z + s) % NZ
            hops = PLUS_HOPS if plus else MINUS_HOPS
            dev = dev_up if plus else dev_down
            for name, h, yy in (("own0", 0, yl), ("own1", 1, yl), ("par1", 1, 1 - yl)):
                if s > hops[name]:
                    continue
                jj = at(zo, yy, c)
                if name == "par1" and s == 4:
                    if plus:
                        x_wait(h, jj)
                        x_send(h, jj, dev_c)
                    continue
                x_wait(h, jj)
                if name == "par1" and s == 3:
                    send_if(c == (0 if plus else 1), xg.at[h, jj], xg.at[h, jj], xr.at[h, jj], dev)
                elif s < hops[name]:
                    x_send(h, jj, dev)
                if name == "own0":
                    x_send(h, jj, dev_y)
                x_send(h, jj, dev_c)

    def x_late(s):
        for zo in ((z + NZ - s) % NZ, (z + s) % NZ)[: 1 if s == NZ // 2 else 2]:
            jj = at(zo, 1 - yl, c)
            x_wait(0, jj)
            x_send(0, jj, dev_c)

    def x_other_core(s):
        for zo in ((z + NZ - s) % NZ, (z + s) % NZ)[: 1 if s in (0, NZ // 2) else 2]:
            for yy in range(2):
                for h in range(2):
                    x_wait(h, at(zo, yy, 1 - c))

    def origin(s, k):
        return (z + NZ - s + k * 2 * s) % NZ

    def n_origins(s):
        return 1 if s in (0, NZ // 2) else 2

    def prepare(s):
        x_other_core(s)

        def body(k, carry):
            zo, h, r = origin(s, k // 8), (k // 4) % 2, k % 4
            rows = pl.ds(pl.multiple_of(r * 128, 128), 128)
            squares = None
            for b in range(4):
                jj = zo * 4 + b
                block = xg[h, jj, rows, :].astype(F32)
                gains = jnp.sum(xg[h, jj, pl.ds(H, 16), :].astype(F32), axis=0, keepdims=True)
                xs[h, zo, rows, b * F:(b + 1) * F] = (block * gains).astype(BF16)
                squares = block * block if squares is None else squares + block * block
            ssq[pl.ds(pl.multiple_of(h * H + r * 128, 128), 128), :] += squares
            return carry

        lax.fori_loop(0, 8 * n_origins(s), body, 0)

    def multiply(s):
        def body(k, carry):
            zo, h = origin(s, k // 2), k % 2
            into = pl.ds(pl.multiple_of(8 + h * H, 8), H)
            right = jnp.concatenate(
                [jnp.concatenate([wg[zo, half, q] for half in range(2)], axis=0) for q in range(3)], axis=1
            )
            product = jnp.dot(xs[h, zo], right, preferred_element_type=F32)
            for q in range(3):
                ext[q, into, :] += product[:, q * F:(q + 1) * F]
            return carry

        lax.fori_loop(0, 2 * n_origins(s), body, 0)

    def o_send(ii, half, dev):
        send(wo.at[ii, half], wo.at[ii, half], wor.at[ii, half, 0], dev)

    def o_wait(ii, half):
        arrived(wo.at[ii, half], wor.at[ii, half, 0])

    pd, pu = (pair + NI - 2) % NI, (pair + 2) % NI
    far, pfar = (i + 4) % NI, (pair + 4) % NI

    def pass_on(wait, forward, below, above):
        for half in (0, 1):
            wait(below, half)
            if half == 0:
                forward(below, 0, dev_xu)
            wait(above, half)
            if half == 1:
                forward(above, 1, dev_xd)

    x_step(1)
    pass_on(w_wait, w_send, ix_down, ix_up)
    prepare(0)
    x_step(2)
    x_late(1)
    pass_on(w_wait, w_send, pd, pu)
    prepare(1)
    for yy, cc in ((yl, 1 - c), (1 - yl, c), (1 - yl, 1 - c)):
        rows = pl.ds(pl.multiple_of(cc * F, F), F)
        arrived(wo.at[i, yy, rows, :], wor.at[i, yy, cc])
    for half in range(2):
        for dev in (dev_yh, dev_xu, dev_xd):
            o_send(i, half, dev)
    x_step(3)
    x_late(2)
    prepare(2)
    for half in range(2):
        w_wait(far, half)
    for half in range(2):
        w_wait(pfar, half)
    multiply(0)
    multiply(1)
    x_step(4)
    for half in range(2):
        o_wait(pair, half)
        for dev in (dev_xu, dev_xd):
            o_send(pair, half, dev)
    x_late(3)
    prepare(3)
    multiply(2)
    x_late(4)
    pass_on(o_wait, o_send, ix_down, ix_up)
    multiply(3)
    prepare(4)
    multiply(4)
    pass_on(o_wait, o_send, pd, pu)

    def normalise(r, carry):
        rows = pl.ds(pl.multiple_of(r * 128, 128), 128)
        into = pl.ds(pl.multiple_of(8 + r * 128, 8), 128)
        total = jnp.sum(ssq[rows, :], axis=1, keepdims=True)
        inverse = lax.rsqrt(total * (1.0 / D) + 1e-06)
        ext[:, into, :] = (ext[:, into, :] * inverse[None]).astype(BF16).astype(F32)
        return carry

    lax.fori_loop(0, T // 128, normalise, 0)
    send_if(i < NI - 1, ext.at[:, pl.ds(T, 8)], ext.at[:, pl.ds(0, 8)], hr, ((i + 1) % NI, j))

    rate_t, resid_t = rate[...], resid[...]
    scale_t = jnp.sqrt(one_minus_exp_neg(2.0 * rate_t))
    weight_t = resid_t * scale_t
    lam_t = jnp.exp(-rate_t)

    def wide(table, n):
        return jnp.broadcast_to(table[n:n + 1, :], (CH, F))

    lam = [wide(lam_t, n) for n in range(ORDER)]
    tap = lambda t, q: jnp.broadcast_to(filt[t, q:q + 1, :], (CH, F))

    @pl.when(i == 0)
    def _():
        ext[:, 6:8, :] = tail[...].astype(F32)

    @pl.when(i > 0)
    def _():
        arrived(ext.at[:, pl.ds(0, 8)], hr)

    def chunk_rows(start, q):
        return ext[q, pl.ds(start, CH, stride=CL), :]

    kt, vt = [tap(t, 1) for t in range(3)], [tap(t, 2) for t in range(3)]
    U = 4

    def first(it, carry):
        k1, k2, v1, v2 = carry[:4]
        state = list(carry[4:])
        for u in range(U):
            s = it * U + u
            k0, v0 = chunk_rows(8 + s, 1), chunk_rows(8 + s, 2)
            keys = kt[0] * k0 + kt[1] * k1 + kt[2] * k2
            values = vt[0] * v0 + vt[1] * v1 + vt[2] * v2
            m = (keys * values).astype(BF16).astype(F32)
            mx[s] = m
            state = [lam[n] * state[n] + m for n in range(ORDER)]
            k1, k2, v1, v2 = k0, k1, v0, v1
        return (k1, k2, v1, v2, *state)

    zero = jnp.zeros((CH, F), F32)
    carry = lax.fori_loop(
        0, CL // U, first,
        (chunk_rows(7, 1), chunk_rows(6, 1), chunk_rows(7, 2), chunk_rows(6, 2)) + (zero,) * ORDER,
    )
    row8 = lax.broadcasted_iota(jnp.int32, (CH, F), 0)
    for n in range(ORDER):
        total, r = carry[4 + n], jnp.broadcast_to(rate_t[n:n + 1, :], (CH, F))
        for shift in (1, 2, 4):
            moved = jnp.where(row8 >= shift, pltpu.roll(total, shift, axis=0), 0.0)
            total = total + jnp.exp(-r * float(CL * shift)) * moved
        ts[n] = total
        endb[n:n + 1, :] = total[CH - 1:CH, :]
    ends[i] = endb[...]
    for k in range(1, NI):
        send(endb, ends.at[i], er.at[i], ((i + k) % NI, j))
    start_t = st_in[...] / scale_t
    whole = jnp.exp(-rate_t * float(T))
    for k in range(1, NI):
        arrived(ends.at[(i + k) % NI], er.at[(i + k) % NI])
    now, mine = start_t, start_t
    for k in range(NI):
        mine = jnp.where(i == k, now, mine)
        now = whole * now + ends[k]
    st_out[...] = now * scale_t

    qt = [tap(t, 0) for t in range(3)]
    weight = [wide(weight_t, n) for n in range(ORDER)]
    direct = jnp.broadcast_to(skip[...], (CH, F))
    chunk_start = row8.astype(F32) * float(CL)
    entering = []
    for n in range(ORDER):
        r = jnp.broadcast_to(rate_t[n:n + 1, :], (CH, F))
        before = jnp.where(row8 >= 1, pltpu.roll(ts[n], 1, axis=0), 0.0)
        entering.append(before + jnp.exp(-r * chunk_start) * jnp.broadcast_to(mine[n:n + 1, :], (CH, F)))

    def second(it, carry):
        q1, q2 = carry[:2]
        state = list(carry[2:])
        for u in range(U):
            s = it * U + u
            q0 = chunk_rows(8 + s, 0)
            query = qt[0] * q0 + qt[1] * q1 + qt[2] * q2
            m = mx[s]
            state = [lam[n] * state[n] + m for n in range(ORDER)]
            terms = [weight[n] * state[n] for n in range(ORDER)] + [direct * m]
            while len(terms) > 1:
                terms = [a + b for a, b in zip(terms[::2], terms[1::2])] + terms[len(terms) & ~1:]
            gf[pl.ds(s, CH, stride=CL), :] = query * terms[0]
            q1, q2 = q0, q1
        return (q1, q2, *state)

    lax.fori_loop(0, CL // U, second, (chunk_rows(7, 0), chunk_rows(6, 0), *entering))

    def g_send(h, yy, dev):
        send(gk.at[h, yy * 2 + c], gk.at[h, yy * 2 + c], gr.at[h, yy * 2 + c], dev)

    def g_wait(h, slot):
        arrived(gk.at[h, slot], gr.at[h, slot])

    for h in range(2):
        gk[h, yl * 2 + c] = gf[h * H:(h + 1) * H, :].astype(BF16)
        g_send(h, yl, dev_y)
        g_send(h, yl, dev_c)
    for half in range(2):
        o_wait(far, half)
        o_wait(pfar, half)
    for h in range(2):
        g_wait(h, (1 - yl) * 2 + c)
        g_send(h, 1 - yl, dev_c)

    def partial(h, first_to, second_to):
        left = jnp.concatenate([gk[h, slot] for slot in range(4)], axis=1)
        right = jnp.concatenate(
            [jnp.concatenate([wo[to, half] for half in range(2)], axis=0) for to in (first_to, second_to)], axis=1
        )
        product = jnp.dot(left, right, preferred_element_type=F32)
        pa[h, first_to] = product[:, 0:F]
        pa[h, second_to] = product[:, F:2 * F]

    steps = {(d, h): 4 if d == h else 3 for d in range(2) for h in range(2)}

    def target(d, h, s):
        n = steps[d, h]
        return (z + n - s) % NZ if d == 0 else (z + NZ - n + s) % NZ

    def pass_sum(d, h, s):
        total = pa[h, target(d, h, s)]
        if s > 0:
            arrived(rb.at[d, h, s - 1], rr.at[d, h, s - 1])
            total = total + rb[d, h, s - 1].astype(F32)
        sb[d, h, s] = total.astype(BF16)
        send(sb.at[d, h, s], rb.at[d, h, s], rr.at[d, h, s], dev_up if d == 0 else dev_down)

    for h in range(2):
        g_wait(h, yl * 2 + 1 - c)
        g_wait(h, (1 - yl) * 2 + 1 - c)
        partial(h, target(0, h, 0), target(1, h, 0))
        pass_sum(0, h, 0)
        pass_sum(1, h, 0)
    for h in range(2):
        partial(h, target(0, h, 1), target(1, h, 1))
    for h in range(2):
        partial(h, target(0, h, 2), target(1, h, 2))
        partial(h, target(h, h, 3), z)
    for s in range(1, 4):
        for h in range(2):
            for d in range(2):
                if s < steps[d, h]:
                    pass_sum(d, h, s)
    for h in range(2):
        rows = slice(h * H, (h + 1) * H)
        total = pa[h, z] + act[rows, :].astype(F32)
        for d in range(2):
            last = steps[d, h] - 1
            arrived(rb.at[d, h, last], rr.at[d, h, last])
            total = total + rb[d, h, last].astype(F32)
        out[rows, :] = total.astype(BF16)

    for copy, cond in sends:
        if cond is None:
            copy.wait_send()
        else:
            pl.when(cond)(lambda copy=copy: copy.wait_send())


def local(activations, norm_gain, w_in, tail_rows, short_filter, decay_rate, residue, skip_gain, state_in, w_out):
    vmem = pl.BlockSpec(memory_space=pltpu.VMEM)
    dma = pltpu.SemaphoreType.DMA
    block_out, state_out = pl.pallas_call(
        block_kernel,
        out_shape=(jax.ShapeDtypeStruct((T, F), BF16), jax.ShapeDtypeStruct((ORDER, F), F32)),
        in_specs=[vmem] * 10,
        out_specs=(vmem, vmem),
        scratch_shapes=[
            pltpu.VMEM((2, NJ, HG, F), BF16),
            pltpu.VMEM((2, NZ, H, 4 * F), BF16),
            pltpu.VMEM((NI, 2, 3, 256, F), BF16),
            pltpu.VMEM((2, 3, 256, F), BF16),
            pltpu.VMEM((3, T + 8, F), F32),
            pltpu.VMEM((T, F), F32),
            pltpu.VMEM((CL, CH, F), F32),
            pltpu.VMEM((ORDER, CH, F), F32),
            pltpu.VMEM((ORDER, F), F32),
            pltpu.VMEM((NI, ORDER, F), F32),
            pltpu.VMEM((T, F), F32),
            pltpu.VMEM((2, 4, H, F), BF16),
            pltpu.VMEM((4, F, F), BF16),
            pltpu.VMEM((NI, 2, 2 * F, F), BF16),
            pltpu.VMEM((2, NZ, H, F), F32),
            pltpu.VMEM((2, 2, 4, H, F), BF16),
            pltpu.VMEM((2, 2, 4, H, F), BF16),
            dma((N_SEND,)),
            dma((2, NJ)),
            dma((NI, 2)),
            dma((2,)),
            dma,
            dma((NI,)),
            dma((NI, 2, 2)),
            dma((2, 4)),
            dma((2, 2, 4)),
        ],
        compiler_params=pltpu.CompilerParams(
            collective_id=0, has_side_effects=True, vmem_limit_bytes=56 << 20
        ),
    )(
        activations, norm_gain.reshape(1, F), w_in.transpose(1, 0, 2), tail_rows.transpose(0, 2, 1), short_filter,
        decay_rate.T, residue.T, skip_gain.reshape(1, F), state_in.T, w_out,
    )
    return block_out, state_out.T


def solution(mesh):
    placed = (
        P("ctx", "mp"),
        P("mp"),
        P("ctx", None, "mp"),
        P(None, "mp", None),
        P(None, None, "mp"),
        P("mp", None),
        P("mp", None),
        P("mp"),
        P("mp", None),
        P("mp", "ctx"),
    )
    return jax.shard_map(
        local, mesh=mesh, in_specs=placed, out_specs=(P("ctx", "mp"), P("mp", None)), check_vma=False
    )
```

```python
import jax
import jax.numpy as jnp
from jax import lax
from jax.experimental import pallas as pl
from jax.experimental.pallas import tpu as pltpu
from jax.sharding import PartitionSpec as P

MESH = pl.DeviceIdType.MESH
F32, BF16 = jnp.float32, jnp.bfloat16

NI, NJ = 8, 32
NZ, NX = 8, 4
T, F, D, ORDER = 1024, 128, 4096, 16
H = T // 2
PARTS = (384, 640)
STARTS = (0, 384)
GAIN_ROWS = 16
CH = 8
CL = T // CH
GROUPS = {name: n for n, name in enumerate(("x0", "x1", "w", "o", "ws", "halo", "ends", "g", "sum"))}
PLUS_HOPS = {"own0": 4, "own1": 3, "par1": 4}
MINUS_HOPS = {"own0": 3, "own1": 4, "par1": 4}


def one_minus_exp_neg(v):
    series = 1.0 - v * (1.0 / 8.0)
    for k in (7, 6, 5, 4, 3, 2):
        series = 1.0 - v * (1.0 / k) * series
    return v * series


def block_kernel(
    act, gain, w_local, tail, filt, rate, resid, skip, st_in, wout,
    out, st_out,
    xg, xs, wg, ext, ssq, mx, ts, endb, ends, gf, gk, ws, wo, pa, sb, rb,
    ssem, xr, wr, hr, er, wor, gr, rr,
):
    i, j = lax.axis_index("ctx"), lax.axis_index("mp")
    z, yl, c = j // 4, (j // 2) % 2, j % 2
    at = lambda zz, yy, cc: zz * 4 + yy * 2 + cc
    up, down = (z + 1) % NZ, (z + NZ - 1) % NZ
    dev_up, dev_down = (i, at(up, yl, c)), (i, at(down, yl, c))
    dev_y, dev_c = (i, at(z, 1 - yl, c)), (i, at(z, yl, 1 - c))
    ix_up, ix_down = (i + 2) % NI, (i + NI - 2) % NI
    pair = i + 1 - 2 * (i % 2)
    dev_xu, dev_xd, dev_yh = (ix_up, j), (ix_down, j), (pair, j)
    dev_xf = ((i + 4) % NI, j)
    dev_yc = (i, at(z, 1 - yl, 1 - c))

    def transfer(group, src, dst, recv_sem, dev):
        return pltpu.make_async_remote_copy(
            src_ref=src, dst_ref=dst, send_sem=ssem.at[GROUPS[group]], recv_sem=recv_sem,
            device_id=dev, device_id_type=MESH,
        )

    counts = dict.fromkeys(GROUPS, 0)

    def send(group, src, dst, recv_sem, dev):
        counts[group] += 1
        transfer(group, src, dst, recv_sem, dev).start()

    def all_sent(group, refs):
        transfer(group, refs, refs, hr, dev_up).wait_send()

    def arrived(dst, recv_sem):
        pltpu.make_async_remote_copy(
            src_ref=dst, dst_ref=dst, send_sem=ssem.at[0], recv_sem=recv_sem,
            device_id=dev_up, device_id_type=MESH,
        ).wait_recv()

    barrier = pltpu.get_barrier_semaphore()

    def tell(dev):
        pl.semaphore_signal(barrier, inc=1, device_id=dev, device_id_type=MESH)

    for dev in (dev_up, dev_down, dev_c, dev_y, dev_yc):
        tell(dev)
    for k in range(1, NI):
        tell(((i + k) % NI, j))

    g = gain[...]
    g_hi = g.astype(BF16)
    g_rest = g - g_hi.astype(F32)
    g_mid = g_rest.astype(BF16)
    g_lo = (g_rest - g_mid.astype(F32)).astype(BF16)
    row16 = lax.broadcasted_iota(jnp.int32, (16, F), 0)
    zero16 = jnp.zeros((16, F), F32)
    g_rows = jnp.where(
        row16 == 0, g_hi.astype(F32) + zero16,
        jnp.where(row16 == 1, g_mid.astype(F32) + zero16,
                  jnp.where(row16 == 2, g_lo.astype(F32) + zero16, zero16)),
    ).astype(BF16)
    for h in range(2):
        xg[h, j, 0:PARTS[h], :] = act[STARTS[h]:STARTS[h] + PARTS[h], :]
        xg[h, j, PARTS[h]:PARTS[h] + GAIN_ROWS, :] = g_rows
    for half in range(2):
        wg[i, half] = w_local[:, half * 256:(half + 1) * 256, :]
    for k in range(4):
        ws[k] = wout[:, k * F:(k + 1) * F]
    wo[i, yl, pl.ds(pl.multiple_of(c * F, F), F), :] = ws[yl * 2 + c]

    pl.semaphore_wait(barrier, 5 + NI - 1)

    def x_part(h, jj):
        return xg.at[h, jj, pl.ds(0, PARTS[h] + GAIN_ROWS), :]

    def x_send(h, jj, dev):
        send(f"x{h}", x_part(h, jj), x_part(h, jj), xr.at[h, jj], dev)

    def x_wait(h, jj):
        arrived(x_part(h, jj), xr.at[h, jj])

    def w_send(ii, half, dev):
        send("w", wg.at[ii, half], wg.at[ii, half], wr.at[ii, half], dev)

    def w_wait(ii, half):
        arrived(wg.at[ii, half], wr.at[ii, half])

    for h in range(2):
        x_send(h, j, dev_y)
        x_send(h, j, dev_up)
        x_send(h, j, dev_down)
        x_send(h, j, dev_c)
    for half in range(2):
        for dev in (dev_yh, dev_xu, dev_xd, dev_xf):
            w_send(i, half, dev)

    mine_rows = pl.ds(pl.multiple_of(c * F, F), F)
    for dev, block in ((dev_c, yl * 2 + 1 - c), (dev_y, (1 - yl) * 2 + c), (dev_yc, (1 - yl) * 2 + 1 - c)):
        send("ws", ws.at[block], wo.at[i, yl, mine_rows, :], wor.at[i, yl, c], dev)

    def clear(r, carry):
        ext[:, pl.ds(8 + r * 128, 128), :] = jnp.zeros((3, 128, F), F32)
        ssq[pl.ds(r * 128, 128), :] = jnp.zeros((128, F), F32)
        return carry

    lax.fori_loop(0, T // 128, clear, 0)

    jp = at(z, 1 - yl, c)
    x_wait(1, jp)
    x_send(1, jp, dev_up)
    x_send(1, jp, dev_down)
    x_send(1, jp, dev_c)
    x_wait(0, jp)
    x_send(0, jp, dev_c)
    for half in range(2):
        w_wait(pair, half)
        for dev in (dev_xu, dev_xd, dev_xf):
            w_send(pair, half, dev)

    def x_step(s):
        for plus in (True, False):
            zo = (z + NZ - s) % NZ if plus else (z + s) % NZ
            hops = PLUS_HOPS if plus else MINUS_HOPS
            dev = dev_up if plus else dev_down
            for name, h, yy in (("own0", 0, yl), ("own1", 1, yl), ("par1", 1, 1 - yl)):
                if s > hops[name]:
                    continue
                jj = at(zo, yy, c)
                if name == "par1" and s == 4:
                    if plus:
                        x_wait(h, jj)
                        x_send(h, jj, dev_c)
                    continue
                x_wait(h, jj)
                if name == "par1" and s == 3:
                    if plus:
                        counts["x1"] += 1
                    pl.when(c == (0 if plus else 1))(
                        transfer("x1", x_part(h, jj), x_part(h, jj), xr.at[h, jj], dev).start
                    )
                elif s < hops[name]:
                    x_send(h, jj, dev)
                if name == "own0":
                    x_send(h, jj, dev_y)
                x_send(h, jj, dev_c)

    def x_late(s):
        for zo in ((z + NZ - s) % NZ, (z + s) % NZ)[: 1 if s == NZ // 2 else 2]:
            jj = at(zo, 1 - yl, c)
            x_wait(0, jj)
            x_send(0, jj, dev_c)

    def x_other_core(s):
        for zo in ((z + NZ - s) % NZ, (z + s) % NZ)[: 1 if s in (0, NZ // 2) else 2]:
            for yy in range(2):
                for h in range(2):
                    x_wait(h, at(zo, yy, 1 - c))

    def origin(s, k):
        return (z + NZ - s + k * 2 * s) % NZ

    def n_origins(s):
        return 1 if s in (0, NZ // 2) else 2

    def prepare(s):
        x_other_core(s)

        def body(k, carry):
            zo, r = origin(s, k // 8), k % 8
            h = (r * 128 + T - STARTS[1]) // T
            rows = pl.ds(pl.multiple_of(r * 128 - h * STARTS[1], 128), 128)
            gain_rows = pl.ds(pl.multiple_of(PARTS[0] + h * (PARTS[1] - PARTS[0]), 16), GAIN_ROWS)
            to = pl.ds(pl.multiple_of(r * 128, 128), 128)
            squares = None
            for b in range(4):
                jj = zo * 4 + b
                block = xg[h, jj, rows, :].astype(F32)
                gains = jnp.sum(xg[h, jj, gain_rows, :].astype(F32), axis=0, keepdims=True)
                xs[zo, to, b * F:(b + 1) * F] = (block * gains).astype(BF16)
                squares = block * block if squares is None else squares + block * block
            ssq[to, :] += squares
            return carry

        lax.fori_loop(0, 8 * n_origins(s), body, 0)

    def multiply(s):
        def body(k, carry):
            zo, h = origin(s, k // 2), k % 2
            into = pl.ds(pl.multiple_of(8 + h * H, 8), H)
            right = jnp.concatenate(
                [jnp.concatenate([wg[zo, half, q] for half in range(2)], axis=0) for q in range(3)], axis=1
            )
            product = jnp.dot(
                xs[zo, pl.ds(pl.multiple_of(h * H, H), H), :], right, preferred_element_type=F32
            )
            for q in range(3):
                ext[q, into, :] += product[:, q * F:(q + 1) * F]
            return carry

        lax.fori_loop(0, 2 * n_origins(s), body, 0)

    def o_send(ii, half, dev):
        send("o", wo.at[ii, half], wo.at[ii, half], wor.at[ii, half, 0], dev)

    def o_wait(ii, half):
        arrived(wo.at[ii, half], wor.at[ii, half, 0])

    others = [(ii + k) % NI for ii in (i, pair) for k in (2, 6, 4)]
    x_step(1)
    prepare(0)
    x_step(2)
    x_late(1)
    prepare(1)
    x_step(3)
    x_late(2)
    for yy, cc in ((yl, 1 - c), (1 - yl, c), (1 - yl, 1 - c)):
        rows = pl.ds(pl.multiple_of(cc * F, F), F)
        arrived(wo.at[i, yy, rows, :], wor.at[i, yy, cc])
    prepare(2)
    for ii in others:
        for half in range(2):
            w_wait(ii, half)
    for half in range(2):
        for dev in (dev_yh, dev_xu, dev_xd, dev_xf):
            o_send(i, half, dev)
    multiply(0)
    multiply(1)
    x_step(4)
    x_late(3)
    for half in range(2):
        o_wait(pair, half)
        for dev in (dev_xu, dev_xd, dev_xf):
            o_send(pair, half, dev)
    prepare(3)
    multiply(2)
    x_late(4)
    multiply(3)
    prepare(4)
    multiply(4)

    def normalise(r, carry):
        rows = pl.ds(pl.multiple_of(r * 128, 128), 128)
        into = pl.ds(pl.multiple_of(8 + r * 128, 8), 128)
        total = jnp.sum(ssq[rows, :], axis=1, keepdims=True)
        inverse = lax.rsqrt(total * (1.0 / D) + 1e-06)
        ext[:, into, :] = (ext[:, into, :] * inverse[None]).astype(BF16).astype(F32)
        return carry

    normalise(T // 128 - 1, 0)
    halo = transfer("halo", ext.at[:, pl.ds(T, 8)], ext.at[:, pl.ds(0, 8)], hr, ((i + 1) % NI, j))
    pl.when(i < NI - 1)(halo.start)
    lax.fori_loop(0, T // 128 - 1, normalise, 0)

    rate_t, resid_t = rate[...], resid[...]
    scale_t = jnp.sqrt(one_minus_exp_neg(2.0 * rate_t))
    weight_t = resid_t * scale_t
    lam_t = jnp.exp(-rate_t)

    def wide(table, n):
        return jnp.broadcast_to(table[n:n + 1, :], (CH, F))

    lam = [wide(lam_t, n) for n in range(ORDER)]
    tap = lambda t, q: jnp.broadcast_to(filt[t, q:q + 1, :], (CH, F))

    def chunk_rows(start, q):
        return ext[q, pl.ds(start, CH, stride=CL), :]

    kt, vt = [tap(t, 1) for t in range(3)], [tap(t, 2) for t in range(3)]

    def mix(k0, k1, k2, v0, v1, v2):
        keys = kt[0] * k0 + kt[1] * k1 + kt[2] * k2
        values = vt[0] * v0 + vt[1] * v1 + vt[2] * v2
        return (keys * values).astype(BF16).astype(F32)

    U = 6

    def first(it, carry):
        k1, k2, v1, v2 = carry[:4]
        state = list(carry[4:])
        for u in range(U):
            s = 2 + it * U + u
            k0, v0 = chunk_rows(8 + s, 1), chunk_rows(8 + s, 2)
            m = mix(k0, k1, k2, v0, v1, v2)
            mx[s] = m
            state = [lam[n] * state[n] + m for n in range(ORDER)]
            k1, k2, v1, v2 = k0, k1, v0, v1
        return (k1, k2, v1, v2, *state)

    zero = jnp.zeros((CH, F), F32)
    state = lax.fori_loop(
        0, (CL - 2) // U, first,
        (chunk_rows(9, 1), chunk_rows(8, 1), chunk_rows(9, 2), chunk_rows(8, 2)) + (zero,) * ORDER,
    )[4:]

    @pl.when(i == 0)
    def _():
        ext[:, 6:8, :] = tail[...].astype(F32)

    @pl.when(i > 0)
    def _():
        arrived(ext.at[:, pl.ds(0, 8)], hr)

    heads = [mix(*(chunk_rows(8 + s - back, q) for q in (1, 2) for back in range(3))) for s in range(2)]
    mx[0], mx[1] = heads
    row8 = lax.broadcasted_iota(jnp.int32, (CH, F), 0)
    for n in range(ORDER):
        r = jnp.broadcast_to(rate_t[n:n + 1, :], (CH, F))
        total = state[n] + jnp.exp(-r * float(CL - 2)) * (lam[n] * heads[0] + heads[1])
        for shift in (1, 2, 4):
            moved = jnp.where(row8 >= shift, pltpu.roll(total, shift, axis=0), 0.0)
            total = total + jnp.exp(-r * float(CL * shift)) * moved
        ts[n] = total
        endb[n:n + 1, :] = total[CH - 1:CH, :]
    ends[i] = endb[...]
    for k in range(1, NI):
        send("ends", endb, ends.at[i], er.at[i], ((i + k) % NI, j))
    start_t = st_in[...] / scale_t
    whole = jnp.exp(-rate_t * float(T))
    for k in range(1, NI):
        arrived(ends.at[(i + k) % NI], er.at[(i + k) % NI])
    now, mine = start_t, start_t
    for k in range(NI):
        mine = jnp.where(i == k, now, mine)
        now = whole * now + ends[k]
    st_out[...] = now * scale_t

    qt = [tap(t, 0) for t in range(3)]
    weight = [wide(weight_t, n) for n in range(ORDER)]
    direct = jnp.broadcast_to(skip[...], (CH, F))
    chunk_start = row8.astype(F32) * float(CL)
    entering = []
    for n in range(ORDER):
        r = jnp.broadcast_to(rate_t[n:n + 1, :], (CH, F))
        before = jnp.where(row8 >= 1, pltpu.roll(ts[n], 1, axis=0), 0.0)
        entering.append(before + jnp.exp(-r * chunk_start) * jnp.broadcast_to(mine[n:n + 1, :], (CH, F)))

    V = 4

    def second(it, carry):
        q1, q2 = carry[:2]
        state = list(carry[2:])
        for u in range(V):
            s = it * V + u
            q0 = chunk_rows(8 + s, 0)
            query = qt[0] * q0 + qt[1] * q1 + qt[2] * q2
            m = mx[s]
            state = [lam[n] * state[n] + m for n in range(ORDER)]
            terms = [weight[n] * state[n] for n in range(ORDER)] + [direct * m]
            while len(terms) > 1:
                terms = [a + b for a, b in zip(terms[::2], terms[1::2])] + terms[len(terms) & ~1:]
            gf[pl.ds(s, CH, stride=CL), :] = query * terms[0]
            q1, q2 = q0, q1
        return (q1, q2, *state)

    lax.fori_loop(0, CL // V, second, (chunk_rows(7, 0), chunk_rows(6, 0), *entering))

    def g_send(h, yy, dev):
        send("g", gk.at[h, yy * 2 + c], gk.at[h, yy * 2 + c], gr.at[h, yy * 2 + c], dev)

    def g_wait(h, slot):
        arrived(gk.at[h, slot], gr.at[h, slot])

    for h in range(2):
        gk[h, yl * 2 + c] = gf[h * H:(h + 1) * H, :].astype(BF16)
        g_send(h, yl, dev_y)
        g_send(h, yl, dev_c)
    for ii in others:
        for half in range(2):
            o_wait(ii, half)
    for h in range(2):
        g_wait(h, (1 - yl) * 2 + c)
        g_send(h, 1 - yl, dev_c)

    def partial(h, first_to, second_to):
        left = jnp.concatenate([gk[h, slot] for slot in range(4)], axis=1)
        right = jnp.concatenate(
            [jnp.concatenate([wo[to, half] for half in range(2)], axis=0) for to in (first_to, second_to)], axis=1
        )
        product = jnp.dot(left, right, preferred_element_type=F32)
        pa[h, first_to] = product[:, 0:F]
        pa[h, second_to] = product[:, F:2 * F]

    steps = {(d, h): 4 if d == h else 3 for d in range(2) for h in range(2)}

    def target(d, h, s):
        n = steps[d, h]
        return (z + n - s) % NZ if d == 0 else (z + NZ - n + s) % NZ

    def pass_sum(d, h, s):
        total = pa[h, target(d, h, s)]
        if s > 0:
            arrived(rb.at[d, h, s - 1], rr.at[d, h, s - 1])
            total = total + rb[d, h, s - 1].astype(F32)
        n = d * 7 + h * steps[d, 0] + s
        sb[n] = total.astype(BF16)
        send("sum", sb.at[n], rb.at[d, h, s], rr.at[d, h, s], dev_up if d == 0 else dev_down)

    for h in range(2):
        g_wait(h, yl * 2 + 1 - c)
        g_wait(h, (1 - yl) * 2 + 1 - c)
        partial(h, target(0, h, 0), target(1, h, 0))
        pass_sum(0, h, 0)
        pass_sum(1, h, 0)
    for h in range(2):
        partial(h, target(0, h, 1), target(1, h, 1))
    for h in range(2):
        partial(h, target(0, h, 2), target(1, h, 2))
        partial(h, target(h, h, 3), z)
    for s in range(1, 4):
        for h in range(2):
            for d in range(2):
                if s < steps[d, h]:
                    pass_sum(d, h, s)
    for h in range(2):
        rows = slice(h * H, (h + 1) * H)
        total = pa[h, z] + act[rows, :].astype(F32)
        for d in range(2):
            last = steps[d, h] - 1
            arrived(rb.at[d, h, last], rr.at[d, h, last])
            total = total + rb[d, h, last].astype(F32)
        out[rows, :] = total.astype(BF16)

    for group, refs in (
        ("x0", xg.at[0, pl.ds(0, counts["x0"]), pl.ds(0, PARTS[0] + GAIN_ROWS), :]),
        ("x1", xg.at[1, pl.ds(0, counts["x1"]), pl.ds(0, PARTS[1] + GAIN_ROWS), :]),
        ("w", wg.at[pl.ds(0, counts["w"] // 2)]),
        ("o", wo.at[pl.ds(0, counts["o"] // 2)]),
        ("ws", ws.at[pl.ds(0, counts["ws"])]),
        ("ends", ends.at[pl.ds(0, counts["ends"])]),
        ("g", gk.at[:, pl.ds(0, counts["g"] // 2)]),
        ("sum", sb.at[pl.ds(0, counts["sum"])]),
    ):
        all_sent(group, refs)
    pl.when(i < NI - 1)(halo.wait_send)


def local(activations, norm_gain, w_in, tail_rows, short_filter, decay_rate, residue, skip_gain, state_in, w_out):
    vmem = pl.BlockSpec(memory_space=pltpu.VMEM)
    dma = pltpu.SemaphoreType.DMA
    block_out, state_out = pl.pallas_call(
        block_kernel,
        out_shape=(jax.ShapeDtypeStruct((T, F), BF16), jax.ShapeDtypeStruct((ORDER, F), F32)),
        in_specs=[vmem] * 10,
        out_specs=(vmem, vmem),
        scratch_shapes=[
            pltpu.VMEM((2, NJ, max(PARTS) + GAIN_ROWS, F), BF16),
            pltpu.VMEM((NZ, T, 4 * F), BF16),
            pltpu.VMEM((NI, 2, 3, 256, F), BF16),
            pltpu.VMEM((3, T + 8, F), F32),
            pltpu.VMEM((T, F), F32),
            pltpu.VMEM((CL, CH, F), F32),
            pltpu.VMEM((ORDER, CH, F), F32),
            pltpu.VMEM((ORDER, F), F32),
            pltpu.VMEM((NI, ORDER, F), F32),
            pltpu.VMEM((T, F), F32),
            pltpu.VMEM((2, 4, H, F), BF16),
            pltpu.VMEM((4, F, F), BF16),
            pltpu.VMEM((NI, 2, 2 * F, F), BF16),
            pltpu.VMEM((2, NZ, H, F), F32),
            pltpu.VMEM((14, H, F), BF16),
            pltpu.VMEM((2, 2, 4, H, F), BF16),
            dma((len(GROUPS),)),
            dma((2, NJ)),
            dma((NI, 2)),
            dma,
            dma((NI,)),
            dma((NI, 2, 2)),
            dma((2, 4)),
            dma((2, 2, 4)),
        ],
        compiler_params=pltpu.CompilerParams(
            collective_id=0, has_side_effects=True, vmem_limit_bytes=56 << 20
        ),
    )(
        activations, norm_gain.reshape(1, F), w_in.transpose(1, 0, 2), tail_rows.transpose(0, 2, 1), short_filter,
        decay_rate.T, residue.T, skip_gain.reshape(1, F), state_in.T, w_out,
    )
    return block_out, state_out.T


def solution(mesh):
    placed = (
        P("ctx", "mp"),
        P("mp"),
        P("ctx", None, "mp"),
        P(None, "mp", None),
        P(None, None, "mp"),
        P("mp", None),
        P("mp", None),
        P("mp"),
        P("mp", None),
        P("mp", "ctx"),
    )
    return jax.shard_map(
        local, mesh=mesh, in_specs=placed, out_specs=(P("ctx", "mp"), P("mp", None)), check_vma=False
    )
```

```python
import jax
import jax.numpy as jnp
from jax import lax
from jax.experimental import pallas as pl
from jax.experimental.pallas import tpu as pltpu
from jax.sharding import PartitionSpec as P

MESH = pl.DeviceIdType.MESH
F32, BF16 = jnp.float32, jnp.bfloat16

NI, NJ = 8, 32
NZ, NX = 8, 4
T, F, D, ORDER = 1024, 128, 4096, 16
H = T // 2
PARTS = (448, 576)
STARTS = (0, 448)
GAIN_ROWS = 16
CH = 8
CL = T // CH
NP = 4
PR = CL // NP
PT = T // NP
GROUPS = {name: n for n, name in enumerate(("x0", "x1", "w", "o", "ws", "halo", "ends", "g", "sum"))}
PLUS_HOPS = {"own0": 4, "own1": 3, "par1": 4}
MINUS_HOPS = {"own0": 3, "own1": 4, "par1": 4}


def one_minus_exp_neg(v):
    series = 1.0 - v * (1.0 / 8.0)
    for k in (7, 6, 5, 4, 3, 2):
        series = 1.0 - v * (1.0 / k) * series
    return v * series


def block_kernel(
    act, gain, w_local, tail, filt, rate, resid, skip, st_in, wout,
    out, st_out,
    xg, xs, wg, ext, ssq, mx, ts, endb, ends, gf, gk, ws, wo, pa, sb, rb,
    ssem, xr, wr, hr, er, wor, gr, rr,
):
    i, j = lax.axis_index("ctx"), lax.axis_index("mp")
    z, yl, c = j // 4, (j // 2) % 2, j % 2
    at = lambda zz, yy, cc: zz * 4 + yy * 2 + cc
    up, down = (z + 1) % NZ, (z + NZ - 1) % NZ
    dev_up, dev_down = (i, at(up, yl, c)), (i, at(down, yl, c))
    dev_y, dev_c = (i, at(z, 1 - yl, c)), (i, at(z, yl, 1 - c))
    ix_up, ix_down = (i + 2) % NI, (i + NI - 2) % NI
    pair = i + 1 - 2 * (i % 2)
    dev_xu, dev_xd, dev_yh = (ix_up, j), (ix_down, j), (pair, j)
    dev_xf = ((i + 4) % NI, j)
    dev_yc = (i, at(z, 1 - yl, 1 - c))

    def transfer(group, src, dst, recv_sem, dev):
        return pltpu.make_async_remote_copy(
            src_ref=src, dst_ref=dst, send_sem=ssem.at[GROUPS[group]], recv_sem=recv_sem,
            device_id=dev, device_id_type=MESH,
        )

    counts = dict.fromkeys(GROUPS, 0)

    def send(group, src, dst, recv_sem, dev):
        counts[group] += 1
        transfer(group, src, dst, recv_sem, dev).start()

    def all_sent(group, refs):
        transfer(group, refs, refs, hr, dev_up).wait_send()

    def arrived(dst, recv_sem):
        pltpu.make_async_remote_copy(
            src_ref=dst, dst_ref=dst, send_sem=ssem.at[0], recv_sem=recv_sem,
            device_id=dev_up, device_id_type=MESH,
        ).wait_recv()

    barrier = pltpu.get_barrier_semaphore()

    def tell(dev):
        pl.semaphore_signal(barrier, inc=1, device_id=dev, device_id_type=MESH)

    for dev in (dev_up, dev_down, dev_c, dev_y, dev_yc):
        tell(dev)
    for k in range(1, NI):
        tell(((i + k) % NI, j))

    g = gain[...]
    g_hi = g.astype(BF16)
    g_rest = g - g_hi.astype(F32)
    g_mid = g_rest.astype(BF16)
    g_lo = (g_rest - g_mid.astype(F32)).astype(BF16)
    row16 = lax.broadcasted_iota(jnp.int32, (16, F), 0)
    zero16 = jnp.zeros((16, F), F32)
    g_rows = jnp.where(
        row16 == 0, g_hi.astype(F32) + zero16,
        jnp.where(row16 == 1, g_mid.astype(F32) + zero16,
                  jnp.where(row16 == 2, g_lo.astype(F32) + zero16, zero16)),
    ).astype(BF16)
    for h in range(2):
        xg[h, j, 0:PARTS[h], :] = act[STARTS[h]:STARTS[h] + PARTS[h], :]
        xg[h, j, PARTS[h]:PARTS[h] + GAIN_ROWS, :] = g_rows
    for half in range(2):
        wg[i, half] = w_local[:, half * 256:(half + 1) * 256, :]
    for k in range(4):
        ws[k] = wout[:, k * F:(k + 1) * F]
    wo[i, yl, pl.ds(pl.multiple_of(c * F, F), F), :] = ws[yl * 2 + c]

    pl.semaphore_wait(barrier, 5 + NI - 1)

    def x_part(h, jj):
        return xg.at[h, jj, pl.ds(0, PARTS[h] + GAIN_ROWS), :]

    def x_send(h, jj, dev):
        send(f"x{h}", x_part(h, jj), x_part(h, jj), xr.at[h, jj], dev)

    def x_wait(h, jj):
        arrived(x_part(h, jj), xr.at[h, jj])

    def w_send(ii, half, dev):
        send("w", wg.at[ii, half], wg.at[ii, half], wr.at[ii, half], dev)

    def w_wait(ii, half):
        arrived(wg.at[ii, half], wr.at[ii, half])

    x_send(1, j, dev_y)
    for h in range(2):
        x_send(h, j, dev_up)
        x_send(h, j, dev_down)
    x_send(0, j, dev_y)
    for half in range(2):
        for dev in (dev_xu, dev_xd, dev_xf):
            w_send(i, half, dev)
    for h in range(2):
        x_send(h, j, dev_c)

    mine_rows = pl.ds(pl.multiple_of(c * F, F), F)
    for dev, block in ((dev_c, yl * 2 + 1 - c), (dev_y, (1 - yl) * 2 + c), (dev_yc, (1 - yl) * 2 + 1 - c)):
        send("ws", ws.at[block], wo.at[i, yl, mine_rows, :], wor.at[i, yl, c], dev)

    def clear(r, carry):
        ext[:, pl.ds(8 + r * 128, 128), :] = jnp.zeros((3, 128, F), F32)
        ssq[pl.ds(r * 128, 128), :] = jnp.zeros((128, F), F32)
        return carry

    lax.fori_loop(0, T // 128, clear, 0)

    jp = at(z, 1 - yl, c)
    x_wait(1, jp)
    x_send(1, jp, dev_up)
    x_send(1, jp, dev_down)
    x_send(1, jp, dev_c)
    x_wait(0, jp)
    x_send(0, jp, dev_c)
    for half in range(2):
        w_send(i, half, dev_yh)

    def x_step(s):
        for name, h, yy in (("own0", 0, yl), ("own1", 1, yl), ("par1", 1, 1 - yl)):
            for plus in (True, False):
                zo = (z + NZ - s) % NZ if plus else (z + s) % NZ
                hops = PLUS_HOPS if plus else MINUS_HOPS
                dev = dev_up if plus else dev_down
                if s > hops[name]:
                    continue
                jj = at(zo, yy, c)
                if name == "par1" and s == 4:
                    if plus:
                        x_wait(h, jj)
                        x_send(h, jj, dev_c)
                    continue
                x_wait(h, jj)
                if name == "par1" and s == 3:
                    if plus:
                        counts["x1"] += 1
                    pl.when(c == (0 if plus else 1))(
                        transfer("x1", x_part(h, jj), x_part(h, jj), xr.at[h, jj], dev).start
                    )
                elif s < hops[name]:
                    x_send(h, jj, dev)
                if name == "own0":
                    x_send(h, jj, dev_y)
                x_send(h, jj, dev_c)

    def x_late(s):
        for zo in ((z + NZ - s) % NZ, (z + s) % NZ)[: 1 if s == NZ // 2 else 2]:
            jj = at(zo, 1 - yl, c)
            x_wait(0, jj)
            x_send(0, jj, dev_c)

    def x_other_core(s):
        for zo in ((z + NZ - s) % NZ, (z + s) % NZ)[: 1 if s in (0, NZ // 2) else 2]:
            for yy in range(2):
                for h in range(2):
                    x_wait(h, at(zo, yy, 1 - c))

    def origin(s, k):
        return (z + NZ - s + k * 2 * s) % NZ

    def n_origins(s):
        return 1 if s in (0, NZ // 2) else 2

    def prepare(s):
        x_other_core(s)

        def body(k, carry):
            zo, r = origin(s, k // 16), k % 16
            h = (r * 64 + T - STARTS[1]) // T
            rows = pl.ds(pl.multiple_of(r * 64 - h * STARTS[1], 64), 64)
            gain_rows = pl.ds(pl.multiple_of(PARTS[0] + h * (PARTS[1] - PARTS[0]), 16), GAIN_ROWS)
            to = pl.ds(pl.multiple_of(r * 64, 64), 64)
            squares = None
            for b in range(4):
                jj = zo * 4 + b
                block = xg[h, jj, rows, :].astype(F32)
                gains = jnp.sum(xg[h, jj, gain_rows, :].astype(F32), axis=0, keepdims=True)
                xs[zo, to, b * F:(b + 1) * F] = (block * gains).astype(BF16)
                squares = block * block if squares is None else squares + block * block
            ssq[to, :] += squares
            return carry

        lax.fori_loop(0, 16 * n_origins(s), body, 0)

    def multiply(s):
        origins = [origin(s, k) for k in range(n_origins(s))]

        def body(h, carry):
            into = pl.ds(pl.multiple_of(8 + h * H, 8), H)
            rows = pl.ds(pl.multiple_of(h * H, H), H)
            left = jnp.concatenate([xs[zo, rows, :] for zo in origins], axis=1)
            right = jnp.concatenate(
                [
                    jnp.concatenate([wg[zo, half, q] for zo in origins for half in range(2)], axis=0)
                    for q in range(3)
                ],
                axis=1,
            )
            product = jnp.dot(left, right, preferred_element_type=F32)
            for q in range(3):
                ext[q, into, :] += product[:, q * F:(q + 1) * F]
            return carry

        lax.fori_loop(0, 2, body, 0)

    def o_send(ii, half, dev):
        send("o", wo.at[ii, half], wo.at[ii, half], wor.at[ii, half, 0], dev)

    def o_wait(ii, half):
        arrived(wo.at[ii, half], wor.at[ii, half, 0])

    others = [(ii + k) % NI for ii in (i, pair) for k in (2, 6, 4)]
    x_step(1)
    for half in range(2):
        w_wait(pair, half)
        for dev in (dev_xu, dev_xd, dev_xf):
            w_send(pair, half, dev)
    prepare(0)
    x_step(2)
    x_late(1)
    prepare(1)
    x_step(3)
    x_late(2)
    for yy, cc in ((yl, 1 - c), (1 - yl, c), (1 - yl, 1 - c)):
        rows = pl.ds(pl.multiple_of(cc * F, F), F)
        arrived(wo.at[i, yy, rows, :], wor.at[i, yy, cc])
    prepare(2)
    for ii in others:
        for half in range(2):
            w_wait(ii, half)
    multiply(0)
    multiply(1)
    multiply(2)
    x_step(4)
    x_late(3)
    prepare(3)
    for half in range(2):
        for dev in (dev_yh, dev_xu, dev_xd, dev_xf):
            o_send(i, half, dev)
    multiply(3)
    x_late(4)
    prepare(4)
    multiply(4)

    def normalise(r, carry):
        rows = pl.ds(pl.multiple_of(r * 128, 128), 128)
        into = pl.ds(pl.multiple_of(8 + r * 128, 8), 128)
        total = jnp.sum(ssq[rows, :], axis=1, keepdims=True)
        inverse = lax.rsqrt(total * (1.0 / D) + 1e-06)
        ext[:, into, :] = (ext[:, into, :] * inverse[None]).astype(BF16).astype(F32)
        return carry

    normalise(T // 128 - 1, 0)
    halo = transfer("halo", ext.at[:, pl.ds(T, 8)], ext.at[:, pl.ds(0, 8)], hr, ((i + 1) % NI, j))
    pl.when(i < NI - 1)(halo.start)
    lax.fori_loop(0, T // 128 - 1, normalise, 0)

    rate_t, resid_t = rate[...], resid[...]
    scale_t = jnp.sqrt(one_minus_exp_neg(2.0 * rate_t))
    weight_t = resid_t * scale_t
    lam_t = jnp.exp(-rate_t)

    def wide(table, n):
        return jnp.broadcast_to(table[n:n + 1, :], (CH, F))

    lam = [wide(lam_t, n) for n in range(ORDER)]
    tap = lambda t, q: jnp.broadcast_to(filt[t, q:q + 1, :], (CH, F))

    def chunk_rows(start, q):
        return ext[q, pl.ds(start, CH, stride=CL), :]

    kt, vt = [tap(t, 1) for t in range(3)], [tap(t, 2) for t in range(3)]

    def mix(k0, k1, k2, v0, v1, v2):
        keys = kt[0] * k0 + kt[1] * k1 + kt[2] * k2
        values = vt[0] * v0 + vt[1] * v1 + vt[2] * v2
        return (keys * values).astype(BF16).astype(F32)

    U = 6

    def first(it, carry):
        k1, k2, v1, v2 = carry[:4]
        state = list(carry[4:])
        for u in range(U):
            s = 2 + it * U + u
            k0, v0 = chunk_rows(8 + s, 1), chunk_rows(8 + s, 2)
            m = mix(k0, k1, k2, v0, v1, v2)
            mx[s] = m
            state = [lam[n] * state[n] + m for n in range(ORDER)]
            k1, k2, v1, v2 = k0, k1, v0, v1
        return (k1, k2, v1, v2, *state)

    zero = jnp.zeros((CH, F), F32)
    state = lax.fori_loop(
        0, (CL - 2) // U, first,
        (chunk_rows(9, 1), chunk_rows(8, 1), chunk_rows(9, 2), chunk_rows(8, 2)) + (zero,) * ORDER,
    )[4:]

    @pl.when(i == 0)
    def _():
        ext[:, 6:8, :] = tail[...].astype(F32)

    @pl.when(i > 0)
    def _():
        arrived(ext.at[:, pl.ds(0, 8)], hr)

    heads = [mix(*(chunk_rows(8 + s - back, q) for q in (1, 2) for back in range(3))) for s in range(2)]
    mx[0], mx[1] = heads
    row8 = lax.broadcasted_iota(jnp.int32, (CH, F), 0)
    for n in range(ORDER):
        r = jnp.broadcast_to(rate_t[n:n + 1, :], (CH, F))
        total = state[n] + jnp.exp(-r * float(CL - 2)) * (lam[n] * heads[0] + heads[1])
        for shift in (1, 2, 4):
            moved = jnp.where(row8 >= shift, pltpu.roll(total, shift, axis=0), 0.0)
            total = total + jnp.exp(-r * float(CL * shift)) * moved
        ts[n] = total
        endb[n:n + 1, :] = total[CH - 1:CH, :]
    ends[i] = endb[...]
    for k in range(1, NI):
        send("ends", endb, ends.at[i], er.at[i], ((i + k) % NI, j))
    for half in range(2):
        o_wait(pair, half)
        for dev in (dev_xu, dev_xd, dev_xf):
            o_send(pair, half, dev)
    start_t = st_in[...] / scale_t
    whole = jnp.exp(-rate_t * float(T))
    for k in range(1, NI):
        arrived(ends.at[(i + k) % NI], er.at[(i + k) % NI])
    now, mine = start_t, start_t
    for k in range(NI):
        mine = jnp.where(i == k, now, mine)
        now = whole * now + ends[k]
    st_out[...] = now * scale_t

    qt = [tap(t, 0) for t in range(3)]
    weight = [wide(weight_t, n) for n in range(ORDER)]
    direct = jnp.broadcast_to(skip[...], (CH, F))
    chunk_start = row8.astype(F32) * float(CL)
    entering = []
    for n in range(ORDER):
        r = jnp.broadcast_to(rate_t[n:n + 1, :], (CH, F))
        before = jnp.where(row8 >= 1, pltpu.roll(ts[n], 1, axis=0), 0.0)
        entering.append(before + jnp.exp(-r * chunk_start) * jnp.broadcast_to(mine[n:n + 1, :], (CH, F)))

    V = 4

    def second(it, carry):
        q1, q2 = carry[:2]
        state = list(carry[2:])
        for u in range(V):
            s = it * V + u
            q0 = chunk_rows(8 + s, 0)
            query = qt[0] * q0 + qt[1] * q1 + qt[2] * q2
            m = mx[s]
            state = [lam[n] * state[n] + m for n in range(ORDER)]
            terms = [weight[n] * state[n] for n in range(ORDER)] + [direct * m]
            while len(terms) > 1:
                terms = [a + b for a, b in zip(terms[::2], terms[1::2])] + terms[len(terms) & ~1:]
            gf[pl.ds(s, CH, stride=CL), :] = query * terms[0]
            q1, q2 = q0, q1
        return (q1, q2, *state)

    def g_send(p, yy, dev):
        send("g", gk.at[p, yy * 2 + c], gk.at[p, yy * 2 + c], gr.at[p, yy * 2 + c], dev)

    def g_wait(p, slot):
        arrived(gk.at[p, slot], gr.at[p, slot])

    carry = (chunk_rows(7, 0), chunk_rows(6, 0), *entering)
    for p in range(NP):
        carry = lax.fori_loop(p * PR // V, (p + 1) * PR // V, second, carry)
        for k in range(CH):
            start = k * CL + p * PR
            gk[p, yl * 2 + c, k * PR:(k + 1) * PR, :] = gf[start:start + PR, :].astype(BF16)
        g_send(p, yl, dev_y)
        g_send(p, yl, dev_c)
    for p in range(NP):
        g_wait(p, (1 - yl) * 2 + c)
        g_send(p, 1 - yl, dev_c)
        if p == 0:
            for ii in others:
                for half in range(2):
                    o_wait(ii, half)

    def partial(p, first_to, second_to):
        left = jnp.concatenate([gk[p, slot] for slot in range(4)], axis=1)
        right = jnp.concatenate(
            [jnp.concatenate([wo[to, half] for half in range(2)], axis=0) for to in (first_to, second_to)], axis=1
        )
        product = jnp.dot(left, right, preferred_element_type=F32)
        pa[p, first_to] = product[:, 0:F]
        pa[p, second_to] = product[:, F:2 * F]

    steps = {(d, p): 4 if d == p % 2 else 3 for d in range(2) for p in range(NP)}

    def target(d, p, s):
        n = steps[d, p]
        return (z + n - s) % NZ if d == 0 else (z + NZ - n + s) % NZ

    def pass_sum(d, p, s):
        total = pa[p, target(d, p, s)]
        if s > 0:
            arrived(rb.at[d, p, s - 1], rr.at[d, p, s - 1])
            total = total + rb[d, p, s - 1].astype(F32)
        n = counts["sum"]
        sb[n] = total.astype(BF16)
        send("sum", sb.at[n], rb.at[d, p, s], rr.at[d, p, s], dev_up if d == 0 else dev_down)

    for p in range(NP):
        g_wait(p, yl * 2 + 1 - c)
        g_wait(p, (1 - yl) * 2 + 1 - c)
        partial(p, target(0, p, 0), target(1, p, 0))
        pass_sum(0, p, 0)
        pass_sum(1, p, 0)
    for s in range(1, 4):
        for p in range(NP):
            if s < 3:
                partial(p, target(0, p, s), target(1, p, s))
            else:
                partial(p, target(p % 2, p, 3), z)
            for d in range(2):
                if s < steps[d, p]:
                    pass_sum(d, p, s)
    for p in range(NP):
        total = pa[p, z]
        for d in range(2):
            last = steps[d, p] - 1
            arrived(rb.at[d, p, last], rr.at[d, p, last])
            total = total + rb[d, p, last].astype(F32)
        for k in range(CH):
            rows = slice(k * CL + p * PR, k * CL + (p + 1) * PR)
            out[rows, :] = (total[k * PR:(k + 1) * PR, :] + act[rows, :].astype(F32)).astype(BF16)

    for group, refs in (
        ("x0", xg.at[0, pl.ds(0, counts["x0"]), pl.ds(0, PARTS[0] + GAIN_ROWS), :]),
        ("x1", xg.at[1, pl.ds(0, counts["x1"]), pl.ds(0, PARTS[1] + GAIN_ROWS), :]),
        ("w", wg.at[pl.ds(0, counts["w"] // 2)]),
        ("o", wo.at[pl.ds(0, counts["o"] // 2)]),
        ("ws", ws.at[pl.ds(0, counts["ws"])]),
        ("ends", ends.at[pl.ds(0, counts["ends"])]),
        ("g", gk.at[:, pl.ds(0, counts["g"] // NP)]),
        ("sum", sb.at[pl.ds(0, counts["sum"])]),
    ):
        all_sent(group, refs)
    pl.when(i < NI - 1)(halo.wait_send)


def local(activations, norm_gain, w_in, tail_rows, short_filter, decay_rate, residue, skip_gain, state_in, w_out):
    vmem = pl.BlockSpec(memory_space=pltpu.VMEM)
    dma = pltpu.SemaphoreType.DMA
    block_out, state_out = pl.pallas_call(
        block_kernel,
        out_shape=(jax.ShapeDtypeStruct((T, F), BF16), jax.ShapeDtypeStruct((ORDER, F), F32)),
        in_specs=[vmem] * 10,
        out_specs=(vmem, vmem),
        scratch_shapes=[
            pltpu.VMEM((2, NJ, max(PARTS) + GAIN_ROWS, F), BF16),
            pltpu.VMEM((NZ, T, 4 * F), BF16),
            pltpu.VMEM((NI, 2, 3, 256, F), BF16),
            pltpu.VMEM((3, T + 8, F), F32),
            pltpu.VMEM((T, F), F32),
            pltpu.VMEM((CL, CH, F), F32),
            pltpu.VMEM((ORDER, CH, F), F32),
            pltpu.VMEM((ORDER, F), F32),
            pltpu.VMEM((NI, ORDER, F), F32),
            pltpu.VMEM((T, F), F32),
            pltpu.VMEM((NP, 4, PT, F), BF16),
            pltpu.VMEM((4, F, F), BF16),
            pltpu.VMEM((NI, 2, 2 * F, F), BF16),
            pltpu.VMEM((NP, NZ, PT, F), F32),
            pltpu.VMEM((7 * NP, PT, F), BF16),
            pltpu.VMEM((2, NP, 4, PT, F), BF16),
            dma((len(GROUPS),)),
            dma((2, NJ)),
            dma((NI, 2)),
            dma,
            dma((NI,)),
            dma((NI, 2, 2)),
            dma((NP, 4)),
            dma((2, NP, 4)),
        ],
        compiler_params=pltpu.CompilerParams(
            collective_id=0, has_side_effects=True, vmem_limit_bytes=56 << 20
        ),
    )(
        activations, norm_gain.reshape(1, F), w_in.transpose(1, 0, 2), tail_rows.transpose(0, 2, 1), short_filter,
        decay_rate.T, residue.T, skip_gain.reshape(1, F), state_in.T, w_out,
    )
    return block_out, state_out.T


def solution(mesh):
    placed = (
        P("ctx", "mp"),
        P("mp"),
        P("ctx", None, "mp"),
        P(None, "mp", None),
        P(None, None, "mp"),
        P("mp", None),
        P("mp", None),
        P("mp"),
        P("mp", None),
        P("mp", "ctx"),
    )
    return jax.shard_map(
        local, mesh=mesh, in_specs=placed, out_specs=(P("ctx", "mp"), P("mp", None)), check_vma=False
    )
```

```python
import jax
import jax.numpy as jnp
from jax import lax
from jax.experimental import pallas as pl
from jax.experimental.pallas import tpu as pltpu
from jax.sharding import PartitionSpec as P

MESH = pl.DeviceIdType.MESH
F32, BF16 = jnp.float32, jnp.bfloat16

NI, NJ = 8, 32
NZ, NX = 8, 4
T, F, D, ORDER = 1024, 128, 4096, 16
H = T // 2
PARTS = (448, 576)
STARTS = (0, 448)
GAIN_ROWS = 16
CH = 8
CL = T // CH
NP = 4
PR = CL // NP
PT = T // NP
GROUPS = {name: n for n, name in enumerate(("x0", "x1", "w", "o", "ws", "halo", "ends", "g", "sum"))}
PLUS_HOPS = {"own0": 4, "own1": 3, "par1": 4}
MINUS_HOPS = {"own0": 3, "own1": 4, "par1": 4}


def one_minus_exp_neg(v):
    series = 1.0 - v * (1.0 / 8.0)
    for k in (7, 6, 5, 4, 3, 2):
        series = 1.0 - v * (1.0 / k) * series
    return v * series


def block_kernel(
    act, gain, w_local, tail, filt, rate, resid, skip, st_in, wout,
    out, st_out,
    xg, xs, wg, ext, ssq, mx, ts, endb, ends, gf, gk, ws, wo, pa, sb, rb,
    ssem, xr, wr, hr, er, wor, gr, rr,
):
    i, j = lax.axis_index("ctx"), lax.axis_index("mp")
    z, yl, c = j // 4, (j // 2) % 2, j % 2
    at = lambda zz, yy, cc: zz * 4 + yy * 2 + cc
    up, down = (z + 1) % NZ, (z + NZ - 1) % NZ
    dev_up, dev_down = (i, at(up, yl, c)), (i, at(down, yl, c))
    dev_y, dev_c = (i, at(z, 1 - yl, c)), (i, at(z, yl, 1 - c))
    ix_up, ix_down = (i + 2) % NI, (i + NI - 2) % NI
    pair = i + 1 - 2 * (i % 2)
    dev_xu, dev_xd, dev_yh = (ix_up, j), (ix_down, j), (pair, j)
    dev_yc = (i, at(z, 1 - yl, 1 - c))

    def transfer(group, src, dst, recv_sem, dev):
        return pltpu.make_async_remote_copy(
            src_ref=src, dst_ref=dst, send_sem=ssem.at[GROUPS[group]], recv_sem=recv_sem,
            device_id=dev, device_id_type=MESH,
        )

    counts = dict.fromkeys(GROUPS, 0)

    def send(group, src, dst, recv_sem, dev):
        counts[group] += 1
        transfer(group, src, dst, recv_sem, dev).start()

    def all_sent(group, refs):
        transfer(group, refs, refs, hr, dev_up).wait_send()

    def arrived(dst, recv_sem):
        pltpu.make_async_remote_copy(
            src_ref=dst, dst_ref=dst, send_sem=ssem.at[0], recv_sem=recv_sem,
            device_id=dev_up, device_id_type=MESH,
        ).wait_recv()

    barrier = pltpu.get_barrier_semaphore()

    def tell(dev):
        pl.semaphore_signal(barrier, inc=1, device_id=dev, device_id_type=MESH)

    for dev in (dev_up, dev_down, dev_c, dev_y, dev_yc):
        tell(dev)
    for k in range(1, NI):
        tell(((i + k) % NI, j))

    g = gain[...]
    g_hi = g.astype(BF16)
    g_rest = g - g_hi.astype(F32)
    g_mid = g_rest.astype(BF16)
    g_lo = (g_rest - g_mid.astype(F32)).astype(BF16)
    row16 = lax.broadcasted_iota(jnp.int32, (16, F), 0)
    zero16 = jnp.zeros((16, F), F32)
    g_rows = jnp.where(
        row16 == 0, g_hi.astype(F32) + zero16,
        jnp.where(row16 == 1, g_mid.astype(F32) + zero16,
                  jnp.where(row16 == 2, g_lo.astype(F32) + zero16, zero16)),
    ).astype(BF16)
    for h in range(2):
        xg[h, j, 0:PARTS[h], :] = act[STARTS[h]:STARTS[h] + PARTS[h], :]
        xg[h, j, PARTS[h]:PARTS[h] + GAIN_ROWS, :] = g_rows
    for half in range(2):
        wg[i, half] = w_local[:, half * 256:(half + 1) * 256, :]
    for k in range(4):
        ws[k] = wout[:, k * F:(k + 1) * F]
    wo[i, yl, pl.ds(pl.multiple_of(c * F, F), F), :] = ws[yl * 2 + c]

    pl.semaphore_wait(barrier, 5 + NI - 1)

    def x_part(h, jj):
        return xg.at[h, jj, pl.ds(0, PARTS[h] + GAIN_ROWS), :]

    def x_send(h, jj, dev):
        send(f"x{h}", x_part(h, jj), x_part(h, jj), xr.at[h, jj], dev)

    def x_wait(h, jj):
        arrived(x_part(h, jj), xr.at[h, jj])

    def w_send(ii, half, dev):
        send("w", wg.at[ii, half], wg.at[ii, half], wr.at[ii, half], dev)

    def w_wait(ii, half):
        arrived(wg.at[ii, half], wr.at[ii, half])

    x_send(1, j, dev_y)
    for h in range(2):
        x_send(h, j, dev_up)
        x_send(h, j, dev_down)
    x_send(0, j, dev_y)
    for half in range(2):
        for dev in (dev_xu, dev_xd):
            w_send(i, half, dev)
    for h in range(2):
        x_send(h, j, dev_c)

    mine_rows = pl.ds(pl.multiple_of(c * F, F), F)
    for dev, block in ((dev_c, yl * 2 + 1 - c), (dev_y, (1 - yl) * 2 + c), (dev_yc, (1 - yl) * 2 + 1 - c)):
        send("ws", ws.at[block], wo.at[i, yl, mine_rows, :], wor.at[i, yl, c], dev)

    def clear(r, carry):
        ext[:, pl.ds(8 + r * 128, 128), :] = jnp.zeros((3, 128, F), F32)
        ssq[pl.ds(r * 128, 128), :] = jnp.zeros((128, F), F32)
        return carry

    lax.fori_loop(0, T // 128, clear, 0)

    jp = at(z, 1 - yl, c)
    x_wait(1, jp)
    x_send(1, jp, dev_c)
    x_send(1, jp, dev_up)
    x_send(1, jp, dev_down)
    x_wait(0, jp)
    x_send(0, jp, dev_c)
    for half in range(2):
        w_send(i, half, dev_yh)

    def x_step(s):
        for name, h, yy in (("own0", 0, yl), ("own1", 1, yl), ("par1", 1, 1 - yl)):
            for plus in (True, False):
                zo = (z + NZ - s) % NZ if plus else (z + s) % NZ
                hops = PLUS_HOPS if plus else MINUS_HOPS
                dev = dev_up if plus else dev_down
                if s > hops[name]:
                    continue
                jj = at(zo, yy, c)
                if name == "par1" and s == 4:
                    if plus:
                        x_wait(h, jj)
                        x_send(h, jj, dev_c)
                    continue
                x_wait(h, jj)
                x_send(h, jj, dev_c)
                if name == "par1" and s == 3:
                    if plus:
                        counts["x1"] += 1
                    pl.when(c == (0 if plus else 1))(
                        transfer("x1", x_part(h, jj), x_part(h, jj), xr.at[h, jj], dev).start
                    )
                elif s < hops[name]:
                    x_send(h, jj, dev)
                if name == "own0":
                    x_send(h, jj, dev_y)

    def x_late(s):
        for zo in ((z + NZ - s) % NZ, (z + s) % NZ)[: 1 if s == NZ // 2 else 2]:
            jj = at(zo, 1 - yl, c)
            x_wait(0, jj)
            x_send(0, jj, dev_c)

    def x_other_core(s):
        for zo in ((z + NZ - s) % NZ, (z + s) % NZ)[: 1 if s in (0, NZ // 2) else 2]:
            for yy in range(2):
                for h in range(2):
                    x_wait(h, at(zo, yy, 1 - c))

    def origin(s, k):
        return (z + NZ - s + k * 2 * s) % NZ

    def n_origins(s):
        return 1 if s in (0, NZ // 2) else 2

    def prepare(s):
        x_other_core(s)

        def body(k, carry):
            zo, r = origin(s, k // 16), k % 16
            h = (r * 64 + T - STARTS[1]) // T
            rows = pl.ds(pl.multiple_of(r * 64 - h * STARTS[1], 64), 64)
            gain_rows = pl.ds(pl.multiple_of(PARTS[0] + h * (PARTS[1] - PARTS[0]), 16), GAIN_ROWS)
            to = pl.ds(pl.multiple_of(r * 64, 64), 64)
            squares = None
            for b in range(4):
                jj = zo * 4 + b
                block = xg[h, jj, rows, :].astype(F32)
                gains = jnp.sum(xg[h, jj, gain_rows, :].astype(F32), axis=0, keepdims=True)
                xs[zo, to, b * F:(b + 1) * F] = (block * gains).astype(BF16)
                squares = block * block if squares is None else squares + block * block
            ssq[to, :] += squares
            return carry

        lax.fori_loop(0, 16 * n_origins(s), body, 0)

    def multiply(s):
        origins = [origin(s, k) for k in range(n_origins(s))]

        def body(h, carry):
            into = pl.ds(pl.multiple_of(8 + h * H, 8), H)
            rows = pl.ds(pl.multiple_of(h * H, H), H)
            left = jnp.concatenate([xs[zo, rows, :] for zo in origins], axis=1)
            right = jnp.concatenate(
                [
                    jnp.concatenate([wg[zo, half, q] for zo in origins for half in range(2)], axis=0)
                    for q in range(3)
                ],
                axis=1,
            )
            product = jnp.dot(left, right, preferred_element_type=F32)
            for q in range(3):
                ext[q, into, :] += product[:, q * F:(q + 1) * F]
            return carry

        lax.fori_loop(0, 2, body, 0)

    def o_send(ii, half, dev):
        send("o", wo.at[ii, half], wo.at[ii, half], wor.at[ii, half, 0], dev)

    def o_wait(ii, half):
        arrived(wo.at[ii, half], wor.at[ii, half, 0])

    far, pfar = (i + 4) % NI, (pair + 4) % NI
    others = [(ii + k) % NI for ii in (i, pair) for k in (2, 6, 4)]

    def pass_on(wait, forward, block):
        below, above = (block + NI - 2) % NI, (block + 2) % NI
        for half in (0, 1):
            wait(below, half)
            if half == 0:
                forward(below, 0, dev_xu)
            wait(above, half)
            if half == 1:
                forward(above, 1, dev_xd)

    x_step(1)
    for half in range(2):
        w_wait(pair, half)
        for dev in (dev_xu, dev_xd):
            w_send(pair, half, dev)
    pass_on(w_wait, w_send, i)
    prepare(0)
    for yy, cc in ((yl, 1 - c), (1 - yl, c), (1 - yl, 1 - c)):
        rows = pl.ds(pl.multiple_of(cc * F, F), F)
        arrived(wo.at[i, yy, rows, :], wor.at[i, yy, cc])
    for half in range(2):
        o_send(i, half, dev_yh)
    x_step(2)
    x_late(1)
    pass_on(w_wait, w_send, pair)
    prepare(1)
    x_step(3)
    x_late(2)
    prepare(2)
    for ii in (far, pfar):
        for half in range(2):
            w_wait(ii, half)
    for half in range(2):
        for dev in (dev_xu, dev_xd):
            o_send(i, half, dev)
    for half in range(2):
        o_wait(pair, half)
        for dev in (dev_xu, dev_xd):
            o_send(pair, half, dev)
    multiply(0)
    multiply(1)
    multiply(2)
    x_step(4)
    x_late(3)
    prepare(3)
    pass_on(o_wait, o_send, i)
    multiply(3)
    x_late(4)
    prepare(4)
    multiply(4)

    def normalise(r, carry):
        rows = pl.ds(pl.multiple_of(r * 128, 128), 128)
        into = pl.ds(pl.multiple_of(8 + r * 128, 8), 128)
        total = jnp.sum(ssq[rows, :], axis=1, keepdims=True)
        inverse = lax.rsqrt(total * (1.0 / D) + 1e-06)
        ext[:, into, :] = (ext[:, into, :] * inverse[None]).astype(BF16).astype(F32)
        return carry

    normalise(T // 128 - 1, 0)
    halo = transfer("halo", ext.at[:, pl.ds(T, 8)], ext.at[:, pl.ds(0, 8)], hr, ((i + 1) % NI, j))
    pl.when(i < NI - 1)(halo.start)
    lax.fori_loop(0, T // 128 - 1, normalise, 0)

    rate_t, resid_t = rate[...], resid[...]
    scale_t = jnp.sqrt(one_minus_exp_neg(2.0 * rate_t))
    weight_t = resid_t * scale_t
    lam_t = jnp.exp(-rate_t)

    def wide(table, n):
        return jnp.broadcast_to(table[n:n + 1, :], (CH, F))

    lam = [wide(lam_t, n) for n in range(ORDER)]
    tap = lambda t, q: jnp.broadcast_to(filt[t, q:q + 1, :], (CH, F))

    def chunk_rows(start, q):
        return ext[q, pl.ds(start, CH, stride=CL), :]

    kt, vt = [tap(t, 1) for t in range(3)], [tap(t, 2) for t in range(3)]

    def mix(k0, k1, k2, v0, v1, v2):
        keys = kt[0] * k0 + kt[1] * k1 + kt[2] * k2
        values = vt[0] * v0 + vt[1] * v1 + vt[2] * v2
        return (keys * values).astype(BF16).astype(F32)

    U = 6

    def first(it, carry):
        k1, k2, v1, v2 = carry[:4]
        state = list(carry[4:])
        for u in range(U):
            s = 2 + it * U + u
            k0, v0 = chunk_rows(8 + s, 1), chunk_rows(8 + s, 2)
            m = mix(k0, k1, k2, v0, v1, v2)
            mx[s] = m
            state = [lam[n] * state[n] + m for n in range(ORDER)]
            k1, k2, v1, v2 = k0, k1, v0, v1
        return (k1, k2, v1, v2, *state)

    zero = jnp.zeros((CH, F), F32)
    state = lax.fori_loop(
        0, (CL - 2) // U, first,
        (chunk_rows(9, 1), chunk_rows(8, 1), chunk_rows(9, 2), chunk_rows(8, 2)) + (zero,) * ORDER,
    )[4:]

    @pl.when(i == 0)
    def _():
        ext[:, 6:8, :] = tail[...].astype(F32)

    @pl.when(i > 0)
    def _():
        arrived(ext.at[:, pl.ds(0, 8)], hr)

    heads = [mix(*(chunk_rows(8 + s - back, q) for q in (1, 2) for back in range(3))) for s in range(2)]
    mx[0], mx[1] = heads
    row8 = lax.broadcasted_iota(jnp.int32, (CH, F), 0)
    for n in range(ORDER):
        r = jnp.broadcast_to(rate_t[n:n + 1, :], (CH, F))
        total = state[n] + jnp.exp(-r * float(CL - 2)) * (lam[n] * heads[0] + heads[1])
        for shift in (1, 2, 4):
            moved = jnp.where(row8 >= shift, pltpu.roll(total, shift, axis=0), 0.0)
            total = total + jnp.exp(-r * float(CL * shift)) * moved
        ts[n] = total
        endb[n:n + 1, :] = total[CH - 1:CH, :]
    ends[i] = endb[...]
    for k in (3, 5, 4, 1, 7, 2, 6):
        send("ends", endb, ends.at[i], er.at[i], ((i + k) % NI, j))
    start_t = st_in[...] / scale_t
    pass_on(o_wait, o_send, pair)
    whole = jnp.exp(-rate_t * float(T))
    for k in range(1, NI):
        arrived(ends.at[(i + k) % NI], er.at[(i + k) % NI])
    now, mine = start_t, start_t
    for k in range(NI):
        mine = jnp.where(i == k, now, mine)
        now = whole * now + ends[k]
    st_out[...] = now * scale_t

    qt = [tap(t, 0) for t in range(3)]
    weight = [wide(weight_t, n) for n in range(ORDER)]
    direct = jnp.broadcast_to(skip[...], (CH, F))
    chunk_start = row8.astype(F32) * float(CL)
    entering = []
    for n in range(ORDER):
        r = jnp.broadcast_to(rate_t[n:n + 1, :], (CH, F))
        before = jnp.where(row8 >= 1, pltpu.roll(ts[n], 1, axis=0), 0.0)
        entering.append(before + jnp.exp(-r * chunk_start) * jnp.broadcast_to(mine[n:n + 1, :], (CH, F)))

    V = 4

    def second(it, carry):
        q1, q2 = carry[:2]
        state = list(carry[2:])
        for u in range(V):
            s = it * V + u
            q0 = chunk_rows(8 + s, 0)
            query = qt[0] * q0 + qt[1] * q1 + qt[2] * q2
            m = mx[s]
            state = [lam[n] * state[n] + m for n in range(ORDER)]
            terms = [weight[n] * state[n] for n in range(ORDER)] + [direct * m]
            while len(terms) > 1:
                terms = [a + b for a, b in zip(terms[::2], terms[1::2])] + terms[len(terms) & ~1:]
            gf[pl.ds(s, CH, stride=CL), :] = query * terms[0]
            q1, q2 = q0, q1
        return (q1, q2, *state)

    def g_send(p, yy, dev):
        send("g", gk.at[p, yy * 2 + c], gk.at[p, yy * 2 + c], gr.at[p, yy * 2 + c], dev)

    def g_wait(p, slot):
        arrived(gk.at[p, slot], gr.at[p, slot])

    carry = (chunk_rows(7, 0), chunk_rows(6, 0), *entering)
    for p in range(NP):
        carry = lax.fori_loop(p * PR // V, (p + 1) * PR // V, second, carry)
        for k in range(CH):
            start = k * CL + p * PR
            gk[p, yl * 2 + c, k * PR:(k + 1) * PR, :] = gf[start:start + PR, :].astype(BF16)
        g_send(p, yl, dev_y)
        g_send(p, yl, dev_c)
    for p in range(NP):
        g_wait(p, (1 - yl) * 2 + c)
        g_send(p, 1 - yl, dev_c)
        if p == 0:
            for ii in (far, pfar):
                for half in range(2):
                    o_wait(ii, half)

    def partial(p, first_to, second_to):
        left = jnp.concatenate([gk[p, slot] for slot in range(4)], axis=1)
        right = jnp.concatenate(
            [jnp.concatenate([wo[to, half] for half in range(2)], axis=0) for to in (first_to, second_to)], axis=1
        )
        product = jnp.dot(left, right, preferred_element_type=F32)
        pa[p, first_to] = product[:, 0:F]
        pa[p, second_to] = product[:, F:2 * F]

    steps = {(d, p): 4 if d == p % 2 else 3 for d in range(2) for p in range(NP)}

    def target(d, p, s):
        n = steps[d, p]
        return (z + n - s) % NZ if d == 0 else (z + NZ - n + s) % NZ

    def pass_sum(d, p, s):
        total = pa[p, target(d, p, s)]
        if s > 0:
            arrived(rb.at[d, p, s - 1], rr.at[d, p, s - 1])
            total = total + rb[d, p, s - 1].astype(F32)
        n = counts["sum"]
        sb[n] = total.astype(BF16)
        send("sum", sb.at[n], rb.at[d, p, s], rr.at[d, p, s], dev_up if d == 0 else dev_down)

    for p in range(NP):
        g_wait(p, yl * 2 + 1 - c)
        g_wait(p, (1 - yl) * 2 + 1 - c)
        partial(p, target(0, p, 0), target(1, p, 0))
        pass_sum(0, p, 0)
        pass_sum(1, p, 0)
    for s in range(1, 4):
        for p in range(NP):
            if s < 3:
                partial(p, target(0, p, s), target(1, p, s))
            else:
                partial(p, target(p % 2, p, 3), z)
            for d in range(2):
                if s < steps[d, p]:
                    pass_sum(d, p, s)
    for p in range(NP):
        total = pa[p, z]
        for d in range(2):
            last = steps[d, p] - 1
            arrived(rb.at[d, p, last], rr.at[d, p, last])
            total = total + rb[d, p, last].astype(F32)
        for k in range(CH):
            rows = slice(k * CL + p * PR, k * CL + (p + 1) * PR)
            out[rows, :] = (total[k * PR:(k + 1) * PR, :] + act[rows, :].astype(F32)).astype(BF16)

    for group, refs in (
        ("x0", xg.at[0, pl.ds(0, counts["x0"]), pl.ds(0, PARTS[0] + GAIN_ROWS), :]),
        ("x1", xg.at[1, pl.ds(0, counts["x1"]), pl.ds(0, PARTS[1] + GAIN_ROWS), :]),
        ("w", wg.at[pl.ds(0, counts["w"] // 2)]),
        ("o", wo.at[pl.ds(0, counts["o"] // 2)]),
        ("ws", ws.at[pl.ds(0, counts["ws"])]),
        ("ends", ends.at[pl.ds(0, counts["ends"])]),
        ("g", gk.at[:, pl.ds(0, counts["g"] // NP)]),
        ("sum", sb.at[pl.ds(0, counts["sum"])]),
    ):
        all_sent(group, refs)
    pl.when(i < NI - 1)(halo.wait_send)


def local(activations, norm_gain, w_in, tail_rows, short_filter, decay_rate, residue, skip_gain, state_in, w_out):
    vmem = pl.BlockSpec(memory_space=pltpu.VMEM)
    dma = pltpu.SemaphoreType.DMA
    block_out, state_out = pl.pallas_call(
        block_kernel,
        out_shape=(jax.ShapeDtypeStruct((T, F), BF16), jax.ShapeDtypeStruct((ORDER, F), F32)),
        in_specs=[vmem] * 10,
        out_specs=(vmem, vmem),
        scratch_shapes=[
            pltpu.VMEM((2, NJ, max(PARTS) + GAIN_ROWS, F), BF16),
            pltpu.VMEM((NZ, T, 4 * F), BF16),
            pltpu.VMEM((NI, 2, 3, 256, F), BF16),
            pltpu.VMEM((3, T + 8, F), F32),
            pltpu.VMEM((T, F), F32),
            pltpu.VMEM((CL, CH, F), F32),
            pltpu.VMEM((ORDER, CH, F), F32),
            pltpu.VMEM((ORDER, F), F32),
            pltpu.VMEM((NI, ORDER, F), F32),
            pltpu.VMEM((T, F), F32),
            pltpu.VMEM((NP, 4, PT, F), BF16),
            pltpu.VMEM((4, F, F), BF16),
            pltpu.VMEM((NI, 2, 2 * F, F), BF16),
            pltpu.VMEM((NP, NZ, PT, F), F32),
            pltpu.VMEM((7 * NP, PT, F), BF16),
            pltpu.VMEM((2, NP, 4, PT, F), BF16),
            dma((len(GROUPS),)),
            dma((2, NJ)),
            dma((NI, 2)),
            dma,
            dma((NI,)),
            dma((NI, 2, 2)),
            dma((NP, 4)),
            dma((2, NP, 4)),
        ],
        compiler_params=pltpu.CompilerParams(
            collective_id=0, has_side_effects=True, vmem_limit_bytes=56 << 20
        ),
    )(
        activations, norm_gain.reshape(1, F), w_in.transpose(1, 0, 2), tail_rows.transpose(0, 2, 1), short_filter,
        decay_rate.T, residue.T, skip_gain.reshape(1, F), state_in.T, w_out,
    )
    return block_out, state_out.T


def solution(mesh):
    placed = (
        P("ctx", "mp"),
        P("mp"),
        P("ctx", None, "mp"),
        P(None, "mp", None),
        P(None, None, "mp"),
        P("mp", None),
        P("mp", None),
        P("mp"),
        P("mp", None),
        P("mp", "ctx"),
    )
    return jax.shard_map(
        local, mesh=mesh, in_specs=placed, out_specs=(P("ctx", "mp"), P("mp", None)), check_vma=False
    )
```

```python
import jax
import jax.numpy as jnp
from jax import lax
from jax.experimental import pallas as pl
from jax.experimental.pallas import tpu as pltpu
from jax.sharding import PartitionSpec as P

MESH = pl.DeviceIdType.MESH
F32, BF16 = jnp.float32, jnp.bfloat16

NI, NJ = 8, 32
NZ, NX = 8, 4
T, F, D, ORDER = 1024, 128, 4096, 16
H = T // 2
PARTS = (448, 576)
STARTS = (0, 448)
GAIN_ROWS = 16
CH = 8
CL = T // CH
NP = 4
PR = CL // NP
PT = T // NP
GROUPS = {name: n for n, name in enumerate(("x0", "x1", "w", "o", "ws", "halo", "ends", "g", "sum"))}
PLUS_HOPS = {"own0": 4, "own1": 3, "par1": 4}
MINUS_HOPS = {"own0": 3, "own1": 4, "par1": 4}


def one_minus_exp_neg(v):
    series = 1.0 - v * (1.0 / 8.0)
    for k in (7, 6, 5, 4, 3, 2):
        series = 1.0 - v * (1.0 / k) * series
    return v * series


def block_kernel(
    act, gain, w_local, tail, filt, rate, resid, skip, st_in, wout,
    out, st_out,
    xg, xs, wg, ext, ssq, mx, ts, endb, ends, gf, gk, ws, wo, pa, sb, rb,
    ssem, lr, xr, wr, hr, er, wor, gr, rr,
):
    i, j = lax.axis_index("ctx"), lax.axis_index("mp")
    z, yl, c = j // 4, (j // 2) % 2, j % 2
    at = lambda zz, yy, cc: zz * 4 + yy * 2 + cc
    up, down = (z + 1) % NZ, (z + NZ - 1) % NZ
    dev_up, dev_down = (i, at(up, yl, c)), (i, at(down, yl, c))
    dev_y, dev_c = (i, at(z, 1 - yl, c)), (i, at(z, yl, 1 - c))
    ix_up, ix_down = (i + 2) % NI, (i + NI - 2) % NI
    pair = i + 1 - 2 * (i % 2)
    dev_xu, dev_xd, dev_yh = (ix_up, j), (ix_down, j), (pair, j)
    dev_yc = (i, at(z, 1 - yl, 1 - c))

    def transfer(group, src, dst, recv_sem, dev):
        return pltpu.make_async_remote_copy(
            src_ref=src, dst_ref=dst, send_sem=ssem.at[GROUPS[group]], recv_sem=recv_sem,
            device_id=dev, device_id_type=MESH,
        )

    counts = dict.fromkeys(GROUPS, 0)

    def send(group, src, dst, recv_sem, dev):
        counts[group] += 1
        transfer(group, src, dst, recv_sem, dev).start()

    def all_sent(group, refs):
        transfer(group, refs, refs, hr, dev_up).wait_send()

    def arrived(dst, recv_sem):
        pltpu.make_async_remote_copy(
            src_ref=dst, dst_ref=dst, send_sem=ssem.at[0], recv_sem=recv_sem,
            device_id=dev_up, device_id_type=MESH,
        ).wait_recv()

    own = [
        pltpu.make_async_copy(
            act.at[pl.ds(STARTS[h], PARTS[h]), :], xg.at[h, j, pl.ds(0, PARTS[h]), :], lr.at[h]
        )
        for h in range(2)
    ]
    own += [
        pltpu.make_async_copy(w_local.at[:, pl.ds(half * 256, 256), :], wg.at[i, half], lr.at[2 + half])
        for half in range(2)
    ]
    own += [pltpu.make_async_copy(wout.at[:, pl.ds(k * F, F)], ws.at[k], lr.at[4 + k]) for k in range(4)]
    for copy in own:
        copy.start()

    barrier = pltpu.get_barrier_semaphore()

    def tell(dev):
        pl.semaphore_signal(barrier, inc=1, device_id=dev, device_id_type=MESH)

    for dev in (dev_up, dev_down, dev_c, dev_y, dev_yc):
        tell(dev)
    for k in range(1, NI):
        tell(((i + k) % NI, j))

    g = gain[...]
    g_hi = g.astype(BF16)
    g_rest = g - g_hi.astype(F32)
    g_mid = g_rest.astype(BF16)
    g_lo = (g_rest - g_mid.astype(F32)).astype(BF16)
    row16 = lax.broadcasted_iota(jnp.int32, (16, F), 0)
    zero16 = jnp.zeros((16, F), F32)
    g_rows = jnp.where(
        row16 == 0, g_hi.astype(F32) + zero16,
        jnp.where(row16 == 1, g_mid.astype(F32) + zero16,
                  jnp.where(row16 == 2, g_lo.astype(F32) + zero16, zero16)),
    ).astype(BF16)
    for h in range(2):
        xg[h, j, PARTS[h]:PARTS[h] + GAIN_ROWS, :] = g_rows
    pl.semaphore_wait(barrier, 5 + NI - 1)
    for copy in own:
        copy.wait()
    wo[i, yl, pl.ds(pl.multiple_of(c * F, F), F), :] = ws[yl * 2 + c]

    def x_part(h, jj):
        return xg.at[h, jj, pl.ds(0, PARTS[h] + GAIN_ROWS), :]

    def x_send(h, jj, dev):
        send(f"x{h}", x_part(h, jj), x_part(h, jj), xr.at[h, jj], dev)

    def x_wait(h, jj):
        arrived(x_part(h, jj), xr.at[h, jj])

    def w_send(ii, half, dev):
        send("w", wg.at[ii, half], wg.at[ii, half], wr.at[ii, half], dev)

    def w_wait(ii, half):
        arrived(wg.at[ii, half], wr.at[ii, half])

    x_send(1, j, dev_y)
    for h in range(2):
        x_send(h, j, dev_up)
        x_send(h, j, dev_down)
    x_send(0, j, dev_y)
    for half in range(2):
        for dev in (dev_xu, dev_xd):
            w_send(i, half, dev)
    for h in range(2):
        x_send(h, j, dev_c)

    mine_rows = pl.ds(pl.multiple_of(c * F, F), F)
    for dev, block in ((dev_c, yl * 2 + 1 - c), (dev_y, (1 - yl) * 2 + c), (dev_yc, (1 - yl) * 2 + 1 - c)):
        send("ws", ws.at[block], wo.at[i, yl, mine_rows, :], wor.at[i, yl, c], dev)

    def clear(r, carry):
        ext[:, pl.ds(8 + r * 128, 128), :] = jnp.zeros((3, 128, F), F32)
        ssq[pl.ds(r * 128, 128), :] = jnp.zeros((128, F), F32)
        return carry

    lax.fori_loop(0, T // 128, clear, 0)

    jp = at(z, 1 - yl, c)
    x_wait(1, jp)
    x_send(1, jp, dev_c)
    x_send(1, jp, dev_up)
    x_send(1, jp, dev_down)
    x_wait(0, jp)
    x_send(0, jp, dev_c)
    for half in range(2):
        w_send(i, half, dev_yh)

    def x_step(s, names=("own0", "own1", "par1")):
        for name, h, yy in (("own0", 0, yl), ("own1", 1, yl), ("par1", 1, 1 - yl)):
            for plus in (True, False):
                zo = (z + NZ - s) % NZ if plus else (z + s) % NZ
                hops = PLUS_HOPS if plus else MINUS_HOPS
                dev = dev_up if plus else dev_down
                if s > hops[name] or name not in names:
                    continue
                jj = at(zo, yy, c)
                if name == "par1" and s == 4:
                    if plus:
                        x_wait(h, jj)
                        x_send(h, jj, dev_c)
                    continue
                x_wait(h, jj)
                x_send(h, jj, dev_c)
                if name == "par1" and s == 3:
                    if plus:
                        counts["x1"] += 1
                    pl.when(c == (0 if plus else 1))(
                        transfer("x1", x_part(h, jj), x_part(h, jj), xr.at[h, jj], dev).start
                    )
                elif s < hops[name]:
                    x_send(h, jj, dev)
                if name == "own0":
                    x_send(h, jj, dev_y)

    def x_late(s):
        for zo in ((z + NZ - s) % NZ, (z + s) % NZ)[: 1 if s == NZ // 2 else 2]:
            jj = at(zo, 1 - yl, c)
            x_wait(0, jj)
            x_send(0, jj, dev_c)

    def x_other_core(s):
        for zo in ((z + NZ - s) % NZ, (z + s) % NZ)[: 1 if s in (0, NZ // 2) else 2]:
            for yy in range(2):
                for h in range(2):
                    x_wait(h, at(zo, yy, 1 - c))

    def origin(s, k):
        return (z + NZ - s + k * 2 * s) % NZ

    def n_origins(s):
        return 1 if s in (0, NZ // 2) else 2

    def prepare(s):
        x_other_core(s)

        def body(k, carry):
            zo, r = origin(s, k // 16), k % 16
            h = (r * 64 + T - STARTS[1]) // T
            rows = pl.ds(pl.multiple_of(r * 64 - h * STARTS[1], 64), 64)
            gain_rows = pl.ds(pl.multiple_of(PARTS[0] + h * (PARTS[1] - PARTS[0]), 16), GAIN_ROWS)
            to = pl.ds(pl.multiple_of(r * 64, 64), 64)
            squares = None
            for b in range(4):
                jj = zo * 4 + b
                block = xg[h, jj, rows, :].astype(F32)
                gains = jnp.sum(xg[h, jj, gain_rows, :].astype(F32), axis=0, keepdims=True)
                xs[zo, to, b * F:(b + 1) * F] = (block * gains).astype(BF16)
                squares = block * block if squares is None else squares + block * block
            ssq[to, :] += squares
            return carry

        lax.fori_loop(0, 16 * n_origins(s), body, 0)

    def multiply(s):
        origins = [origin(s, k) for k in range(n_origins(s))]

        def body(h, carry):
            into = pl.ds(pl.multiple_of(8 + h * H, 8), H)
            rows = pl.ds(pl.multiple_of(h * H, H), H)
            left = jnp.concatenate([xs[zo, rows, :] for zo in origins], axis=1)
            right = jnp.concatenate(
                [
                    jnp.concatenate([wg[zo, half, q] for zo in origins for half in range(2)], axis=0)
                    for q in range(3)
                ],
                axis=1,
            )
            product = jnp.dot(left, right, preferred_element_type=F32)
            for q in range(3):
                ext[q, into, :] += product[:, q * F:(q + 1) * F]
            return carry

        lax.fori_loop(0, 2, body, 0)

    def o_send(ii, half, dev):
        send("o", wo.at[ii, half], wo.at[ii, half], wor.at[ii, half, 0], dev)

    def o_wait(ii, half):
        arrived(wo.at[ii, half], wor.at[ii, half, 0])

    far, pfar = (i + 4) % NI, (pair + 4) % NI
    others = [(ii + k) % NI for ii in (i, pair) for k in (2, 6, 4)]

    def pass_on(wait, forward, block):
        below, above = (block + NI - 2) % NI, (block + 2) % NI
        for half in (0, 1):
            wait(below, half)
            if half == 0:
                forward(below, 0, dev_xu)
            wait(above, half)
            if half == 1:
                forward(above, 1, dev_xd)

    x_step(1)
    for half in range(2):
        w_wait(pair, half)
        for dev in (dev_xu, dev_xd):
            w_send(pair, half, dev)
    pass_on(w_wait, w_send, i)
    prepare(0)
    for yy, cc in ((yl, 1 - c), (1 - yl, c), (1 - yl, 1 - c)):
        rows = pl.ds(pl.multiple_of(cc * F, F), F)
        arrived(wo.at[i, yy, rows, :], wor.at[i, yy, cc])
    for half in range(2):
        o_send(i, half, dev_yh)
    x_step(2)
    x_late(1)
    pass_on(w_wait, w_send, pair)
    prepare(1)
    x_step(3)
    x_late(2)
    prepare(2)
    for ii in (far, pfar):
        for half in range(2):
            w_wait(ii, half)
    for half in range(2):
        for dev in (dev_xu, dev_xd):
            o_send(i, half, dev)
    for half in range(2):
        o_wait(pair, half)
        for dev in (dev_xu, dev_xd):
            o_send(pair, half, dev)
    multiply(0)
    x_step(4, ("own0",))
    multiply(1)
    x_step(4, ("own1", "par1"))
    multiply(2)
    x_late(3)
    prepare(3)
    pass_on(o_wait, o_send, i)
    x_late(4)
    multiply(3)
    prepare(4)
    multiply(4)

    def normalise(r, carry):
        rows = pl.ds(pl.multiple_of(r * 128, 128), 128)
        into = pl.ds(pl.multiple_of(8 + r * 128, 8), 128)
        total = jnp.sum(ssq[rows, :], axis=1, keepdims=True)
        inverse = lax.rsqrt(total * (1.0 / D) + 1e-06)
        ext[:, into, :] = (ext[:, into, :] * inverse[None]).astype(BF16).astype(F32)
        return carry

    normalise(T // 128 - 1, 0)
    halo = transfer("halo", ext.at[:, pl.ds(T, 8)], ext.at[:, pl.ds(0, 8)], hr, ((i + 1) % NI, j))
    pl.when(i < NI - 1)(halo.start)
    lax.fori_loop(0, T // 128 - 1, normalise, 0)

    rate_t, resid_t = rate[...], resid[...]
    scale_t = jnp.sqrt(one_minus_exp_neg(2.0 * rate_t))
    weight_t = resid_t * scale_t
    lam_t = jnp.exp(-rate_t)

    def wide(table, n):
        return jnp.broadcast_to(table[n:n + 1, :], (CH, F))

    lam = [wide(lam_t, n) for n in range(ORDER)]
    tap = lambda t, q: jnp.broadcast_to(filt[t, q:q + 1, :], (CH, F))

    def chunk_rows(start, q):
        return ext[q, pl.ds(start, CH, stride=CL), :]

    kt, vt = [tap(t, 1) for t in range(3)], [tap(t, 2) for t in range(3)]

    def mix(k0, k1, k2, v0, v1, v2):
        keys = kt[0] * k0 + kt[1] * k1 + kt[2] * k2
        values = vt[0] * v0 + vt[1] * v1 + vt[2] * v2
        return (keys * values).astype(BF16).astype(F32)

    U = 6

    def first(it, carry):
        k1, k2, v1, v2 = carry[:4]
        state = list(carry[4:])
        for u in range(U):
            s = 2 + it * U + u
            k0, v0 = chunk_rows(8 + s, 1), chunk_rows(8 + s, 2)
            m = mix(k0, k1, k2, v0, v1, v2)
            mx[s] = m
            state = [lam[n] * state[n] + m for n in range(ORDER)]
            k1, k2, v1, v2 = k0, k1, v0, v1
        return (k1, k2, v1, v2, *state)

    zero = jnp.zeros((CH, F), F32)
    state = lax.fori_loop(
        0, (CL - 2) // U, first,
        (chunk_rows(9, 1), chunk_rows(8, 1), chunk_rows(9, 2), chunk_rows(8, 2)) + (zero,) * ORDER,
    )[4:]

    @pl.when(i == 0)
    def _():
        ext[:, 6:8, :] = tail[...].astype(F32)

    @pl.when(i > 0)
    def _():
        arrived(ext.at[:, pl.ds(0, 8)], hr)

    heads = [mix(*(chunk_rows(8 + s - back, q) for q in (1, 2) for back in range(3))) for s in range(2)]
    mx[0], mx[1] = heads
    row8 = lax.broadcasted_iota(jnp.int32, (CH, F), 0)
    for n in range(ORDER):
        r = jnp.broadcast_to(rate_t[n:n + 1, :], (CH, F))
        total = state[n] + jnp.exp(-r * float(CL - 2)) * (lam[n] * heads[0] + heads[1])
        for shift in (1, 2, 4):
            moved = jnp.where(row8 >= shift, pltpu.roll(total, shift, axis=0), 0.0)
            total = total + jnp.exp(-r * float(CL * shift)) * moved
        ts[n] = total
        endb[n:n + 1, :] = total[CH - 1:CH, :]
    ends[i] = endb[...]
    for k in (3, 5, 4, 1, 7, 2, 6):
        send("ends", endb, ends.at[i], er.at[i], ((i + k) % NI, j))
    start_t = st_in[...] / scale_t
    pass_on(o_wait, o_send, pair)
    whole = jnp.exp(-rate_t * float(T))
    for k in range(1, NI):
        arrived(ends.at[(i + k) % NI], er.at[(i + k) % NI])
    now, mine = start_t, start_t
    for k in range(NI):
        mine = jnp.where(i == k, now, mine)
        now = whole * now + ends[k]
    st_out[...] = now * scale_t

    qt = [tap(t, 0) for t in range(3)]
    weight = [wide(weight_t, n) for n in range(ORDER)]
    direct = jnp.broadcast_to(skip[...], (CH, F))
    chunk_start = row8.astype(F32) * float(CL)
    entering = []
    for n in range(ORDER):
        r = jnp.broadcast_to(rate_t[n:n + 1, :], (CH, F))
        before = jnp.where(row8 >= 1, pltpu.roll(ts[n], 1, axis=0), 0.0)
        entering.append(before + jnp.exp(-r * chunk_start) * jnp.broadcast_to(mine[n:n + 1, :], (CH, F)))

    V = 4

    def second(it, carry):
        q1, q2 = carry[:2]
        state = list(carry[2:])
        for u in range(V):
            s = it * V + u
            q0 = chunk_rows(8 + s, 0)
            query = qt[0] * q0 + qt[1] * q1 + qt[2] * q2
            m = mx[s]
            state = [lam[n] * state[n] + m for n in range(ORDER)]
            terms = [weight[n] * state[n] for n in range(ORDER)] + [direct * m]
            while len(terms) > 1:
                terms = [a + b for a, b in zip(terms[::2], terms[1::2])] + terms[len(terms) & ~1:]
            gf[pl.ds(s, CH, stride=CL), :] = query * terms[0]
            q1, q2 = q0, q1
        return (q1, q2, *state)

    def g_send(p, yy, dev):
        send("g", gk.at[p, yy * 2 + c], gk.at[p, yy * 2 + c], gr.at[p, yy * 2 + c], dev)

    def g_wait(p, slot):
        arrived(gk.at[p, slot], gr.at[p, slot])

    carry = (chunk_rows(7, 0), chunk_rows(6, 0), *entering)
    for p in range(NP):
        carry = lax.fori_loop(p * PR // V, (p + 1) * PR // V, second, carry)
        for k in range(CH):
            start = k * CL + p * PR
            gk[p, yl * 2 + c, k * PR:(k + 1) * PR, :] = gf[start:start + PR, :].astype(BF16)
        g_send(p, yl, dev_y)
        g_send(p, yl, dev_c)
    for p in range(NP):
        g_wait(p, (1 - yl) * 2 + c)
        g_send(p, 1 - yl, dev_c)
        if p == 0:
            for ii in (far, pfar):
                for half in range(2):
                    o_wait(ii, half)

    def partial(p, first_to, second_to):
        left = jnp.concatenate([gk[p, slot] for slot in range(4)], axis=1)
        right = jnp.concatenate(
            [jnp.concatenate([wo[to, half] for half in range(2)], axis=0) for to in (first_to, second_to)], axis=1
        )
        product = jnp.dot(left, right, preferred_element_type=F32)
        pa[p, first_to] = product[:, 0:F]
        pa[p, second_to] = product[:, F:2 * F]

    steps = {(d, p): 4 if d == p % 2 else 3 for d in range(2) for p in range(NP)}

    def target(d, p, s):
        n = steps[d, p]
        return (z + n - s) % NZ if d == 0 else (z + NZ - n + s) % NZ

    def pass_sum(d, p, s):
        total = pa[p, target(d, p, s)]
        if s > 0:
            arrived(rb.at[d, p, s - 1], rr.at[d, p, s - 1])
            total = total + rb[d, p, s - 1].astype(F32)
        n = counts["sum"]
        sb[n] = total.astype(BF16)
        send("sum", sb.at[n], rb.at[d, p, s], rr.at[d, p, s], dev_up if d == 0 else dev_down)

    for p in range(NP):
        g_wait(p, yl * 2 + 1 - c)
        g_wait(p, (1 - yl) * 2 + 1 - c)
        partial(p, target(0, p, 0), target(1, p, 0))
        pass_sum(0, p, 0)
        pass_sum(1, p, 0)
    for s in range(1, 4):
        for p in range(NP):
            if s < 3:
                partial(p, target(0, p, s), target(1, p, s))
            else:
                partial(p, target(p % 2, p, 3), z)
            for d in range(2):
                if s < steps[d, p]:
                    pass_sum(d, p, s)
    for p in range(NP):
        total = pa[p, z]
        for d in range(2):
            last = steps[d, p] - 1
            arrived(rb.at[d, p, last], rr.at[d, p, last])
            total = total + rb[d, p, last].astype(F32)
        for k in range(CH):
            start = k * CL + p * PR
            rows = slice(start, start + PR)
            h = int(start >= STARTS[1])
            before = xg[h, j, start - STARTS[h]:start - STARTS[h] + PR, :]
            out[rows, :] = (total[k * PR:(k + 1) * PR, :] + before.astype(F32)).astype(BF16)

    for group, refs in (
        ("x0", xg.at[0, pl.ds(0, counts["x0"]), pl.ds(0, PARTS[0] + GAIN_ROWS), :]),
        ("x1", xg.at[1, pl.ds(0, counts["x1"]), pl.ds(0, PARTS[1] + GAIN_ROWS), :]),
        ("w", wg.at[pl.ds(0, counts["w"] // 2)]),
        ("o", wo.at[pl.ds(0, counts["o"] // 2)]),
        ("ws", ws.at[pl.ds(0, counts["ws"])]),
        ("ends", ends.at[pl.ds(0, counts["ends"])]),
        ("g", gk.at[:, pl.ds(0, counts["g"] // NP)]),
        ("sum", sb.at[pl.ds(0, counts["sum"])]),
    ):
        all_sent(group, refs)
    pl.when(i < NI - 1)(halo.wait_send)


def local(activations, norm_gain, w_in, tail_rows, short_filter, decay_rate, residue, skip_gain, state_in, w_out):
    vmem, anywhere = pl.BlockSpec(memory_space=pltpu.VMEM), pl.BlockSpec(memory_space=pl.ANY)
    dma = pltpu.SemaphoreType.DMA
    block_out, state_out = pl.pallas_call(
        block_kernel,
        out_shape=(jax.ShapeDtypeStruct((T, F), BF16), jax.ShapeDtypeStruct((ORDER, F), F32)),
        in_specs=[anywhere, vmem, anywhere, *[vmem] * 6, anywhere],
        out_specs=(vmem, vmem),
        scratch_shapes=[
            pltpu.VMEM((2, NJ, max(PARTS) + GAIN_ROWS, F), BF16),
            pltpu.VMEM((NZ, T, 4 * F), BF16),
            pltpu.VMEM((NI, 2, 3, 256, F), BF16),
            pltpu.VMEM((3, T + 8, F), F32),
            pltpu.VMEM((T, F), F32),
            pltpu.VMEM((CL, CH, F), F32),
            pltpu.VMEM((ORDER, CH, F), F32),
            pltpu.VMEM((ORDER, F), F32),
            pltpu.VMEM((NI, ORDER, F), F32),
            pltpu.VMEM((T, F), F32),
            pltpu.VMEM((NP, 4, PT, F), BF16),
            pltpu.VMEM((4, F, F), BF16),
            pltpu.VMEM((NI, 2, 2 * F, F), BF16),
            pltpu.VMEM((NP, NZ, PT, F), F32),
            pltpu.VMEM((7 * NP, PT, F), BF16),
            pltpu.VMEM((2, NP, 4, PT, F), BF16),
            dma((len(GROUPS),)),
            dma((8,)),
            dma((2, NJ)),
            dma((NI, 2)),
            dma,
            dma((NI,)),
            dma((NI, 2, 2)),
            dma((NP, 4)),
            dma((2, NP, 4)),
        ],
        compiler_params=pltpu.CompilerParams(
            collective_id=0, has_side_effects=True, vmem_limit_bytes=56 << 20
        ),
    )(
        activations, norm_gain.reshape(1, F), w_in.transpose(1, 0, 2), tail_rows.transpose(0, 2, 1), short_filter,
        decay_rate.T, residue.T, skip_gain.reshape(1, F), state_in.T, w_out,
    )
    return block_out, state_out.T


def solution(mesh):
    placed = (
        P("ctx", "mp"),
        P("mp"),
        P("ctx", None, "mp"),
        P(None, "mp", None),
        P(None, None, "mp"),
        P("mp", None),
        P("mp", None),
        P("mp"),
        P("mp", None),
        P("mp", "ctx"),
    )
    return jax.shard_map(
        local, mesh=mesh, in_specs=placed, out_specs=(P("ctx", "mp"), P("mp", None)), check_vma=False
    )
```

```python
import jax
import jax.numpy as jnp
from jax import lax
from jax.experimental import pallas as pl
from jax.experimental.pallas import tpu as pltpu
from jax.sharding import PartitionSpec as P

MESH = pl.DeviceIdType.MESH
F32, BF16 = jnp.float32, jnp.bfloat16

NI, NJ = 8, 32
NZ, NX = 8, 4
T, F, D, ORDER = 1024, 128, 4096, 16
H = T // 2
PARTS = (448, 576)
STARTS = (0, 448)
GAIN_ROWS = 16
CH = 8
CL = T // CH
NP = 4
PR = CL // NP
PT = T // NP
GROUPS = {name: n for n, name in enumerate(("x0", "x1", "w", "o", "ws", "halo", "ends", "g", "sum"))}
PLUS_HOPS = {"own0": 4, "own1": 3, "par1": 4}
MINUS_HOPS = {"own0": 3, "own1": 4, "par1": 4}


def one_minus_exp_neg(v):
    series = 1.0 - v * (1.0 / 8.0)
    for k in (7, 6, 5, 4, 3, 2):
        series = 1.0 - v * (1.0 / k) * series
    return v * series


def block_kernel(
    act, gain, w_local, tail, filt, rate, resid, skip, st_in, wout,
    out, st_out,
    xg, xs, wg, ext, ssq, mx, ts, endb, ends, gf, gk, ws, wo, pa, sb, rb,
    ssem, lr, xr, wr, hr, er, wor, gr, rr,
):
    i, j = lax.axis_index("ctx"), lax.axis_index("mp")
    z, yl, c = j // 4, (j // 2) % 2, j % 2
    at = lambda zz, yy, cc: zz * 4 + yy * 2 + cc
    up, down = (z + 1) % NZ, (z + NZ - 1) % NZ
    dev_up, dev_down = (i, at(up, yl, c)), (i, at(down, yl, c))
    dev_y, dev_c = (i, at(z, 1 - yl, c)), (i, at(z, yl, 1 - c))
    ix_up, ix_down = (i + 2) % NI, (i + NI - 2) % NI
    pair = i + 1 - 2 * (i % 2)
    dev_xu, dev_xd, dev_yh = (ix_up, j), (ix_down, j), (pair, j)
    dev_yc = (i, at(z, 1 - yl, 1 - c))

    def transfer(group, src, dst, recv_sem, dev):
        return pltpu.make_async_remote_copy(
            src_ref=src, dst_ref=dst, send_sem=ssem.at[GROUPS[group]], recv_sem=recv_sem,
            device_id=dev, device_id_type=MESH,
        )

    counts = dict.fromkeys(GROUPS, 0)

    def send(group, src, dst, recv_sem, dev):
        counts[group] += 1
        transfer(group, src, dst, recv_sem, dev).start()

    def all_sent(group, refs):
        transfer(group, refs, refs, hr, dev_up).wait_send()

    def arrived(dst, recv_sem):
        pltpu.make_async_remote_copy(
            src_ref=dst, dst_ref=dst, send_sem=ssem.at[0], recv_sem=recv_sem,
            device_id=dev_up, device_id_type=MESH,
        ).wait_recv()

    own = [
        pltpu.make_async_copy(
            act.at[pl.ds(STARTS[h], PARTS[h]), :], xg.at[h, j, pl.ds(0, PARTS[h]), :], lr.at[h]
        )
        for h in range(2)
    ]
    own += [
        pltpu.make_async_copy(w_local.at[:, pl.ds(half * 256, 256), :], wg.at[i, half], lr.at[2 + half])
        for half in range(2)
    ]
    own += [pltpu.make_async_copy(wout.at[:, pl.ds(k * F, F)], ws.at[k], lr.at[4 + k]) for k in range(4)]
    for copy in own:
        copy.start()

    barrier = pltpu.get_barrier_semaphore()

    def tell(dev):
        pl.semaphore_signal(barrier, inc=1, device_id=dev, device_id_type=MESH)

    for dev in (dev_up, dev_down, dev_c, dev_y, dev_yc):
        tell(dev)
    for k in range(1, NI):
        tell(((i + k) % NI, j))

    g = gain[...]
    g_hi = g.astype(BF16)
    g_rest = g - g_hi.astype(F32)
    g_mid = g_rest.astype(BF16)
    g_lo = (g_rest - g_mid.astype(F32)).astype(BF16)
    row16 = lax.broadcasted_iota(jnp.int32, (16, F), 0)
    zero16 = jnp.zeros((16, F), F32)
    g_rows = jnp.where(
        row16 == 0, g_hi.astype(F32) + zero16,
        jnp.where(row16 == 1, g_mid.astype(F32) + zero16,
                  jnp.where(row16 == 2, g_lo.astype(F32) + zero16, zero16)),
    ).astype(BF16)
    for h in range(2):
        xg[h, j, PARTS[h]:PARTS[h] + GAIN_ROWS, :] = g_rows
    pl.semaphore_wait(barrier, 5 + NI - 1)
    for copy in own:
        copy.wait()
    wo[i, yl, pl.ds(pl.multiple_of(c * F, F), F), :] = ws[yl * 2 + c]

    def x_part(h, jj):
        return xg.at[h, jj, pl.ds(0, PARTS[h] + GAIN_ROWS), :]

    def x_send(h, jj, dev):
        send(f"x{h}", x_part(h, jj), x_part(h, jj), xr.at[h, jj], dev)

    def x_wait(h, jj):
        arrived(x_part(h, jj), xr.at[h, jj])

    def w_send(ii, half, dev):
        send("w", wg.at[ii, half], wg.at[ii, half], wr.at[ii, half], dev)

    def w_wait(ii, half):
        arrived(wg.at[ii, half], wr.at[ii, half])

    x_send(1, j, dev_y)
    for h in range(2):
        x_send(h, j, dev_up)
        x_send(h, j, dev_down)
    x_send(0, j, dev_y)
    for half in range(2):
        for dev in (dev_xu, dev_xd):
            w_send(i, half, dev)
    for h in range(2):
        x_send(h, j, dev_c)

    mine_rows = pl.ds(pl.multiple_of(c * F, F), F)
    for dev, block in ((dev_c, yl * 2 + 1 - c), (dev_y, (1 - yl) * 2 + c), (dev_yc, (1 - yl) * 2 + 1 - c)):
        send("ws", ws.at[block], wo.at[i, yl, mine_rows, :], wor.at[i, yl, c], dev)

    def clear(r, carry):
        ext[:, pl.ds(8 + r * 128, 128), :] = jnp.zeros((3, 128, F), F32)
        ssq[pl.ds(r * 128, 128), :] = jnp.zeros((128, F), F32)
        return carry

    lax.fori_loop(0, T // 128, clear, 0)

    jp = at(z, 1 - yl, c)
    x_wait(1, jp)
    x_send(1, jp, dev_c)
    x_send(1, jp, dev_up)
    x_send(1, jp, dev_down)
    x_wait(0, jp)
    x_send(0, jp, dev_c)
    for half in range(2):
        w_send(i, half, dev_yh)

    def x_step(s, names=("own0", "own1", "par1")):
        for name, h, yy in (("own0", 0, yl), ("own1", 1, yl), ("par1", 1, 1 - yl)):
            for plus in (True, False):
                zo = (z + NZ - s) % NZ if plus else (z + s) % NZ
                hops = PLUS_HOPS if plus else MINUS_HOPS
                dev = dev_up if plus else dev_down
                if s > hops[name] or name not in names:
                    continue
                jj = at(zo, yy, c)
                if name == "par1" and s == 4:
                    if plus:
                        x_wait(h, jj)
                        x_send(h, jj, dev_c)
                    continue
                x_wait(h, jj)
                x_send(h, jj, dev_c)
                if name == "par1" and s == 3:
                    if plus:
                        counts["x1"] += 1
                    pl.when(c == (0 if plus else 1))(
                        transfer("x1", x_part(h, jj), x_part(h, jj), xr.at[h, jj], dev).start
                    )
                elif s < hops[name]:
                    x_send(h, jj, dev)
                if name == "own0":
                    x_send(h, jj, dev_y)

    def x_late(s):
        for zo in ((z + NZ - s) % NZ, (z + s) % NZ)[: 1 if s == NZ // 2 else 2]:
            jj = at(zo, 1 - yl, c)
            x_wait(0, jj)
            x_send(0, jj, dev_c)

    def x_other_core(s):
        for zo in ((z + NZ - s) % NZ, (z + s) % NZ)[: 1 if s in (0, NZ // 2) else 2]:
            for yy in range(2):
                for h in range(2):
                    x_wait(h, at(zo, yy, 1 - c))

    def origin(s, k):
        return (z + NZ - s + k * 2 * s) % NZ

    def n_origins(s):
        return 1 if s in (0, NZ // 2) else 2

    def prepare(s):
        x_other_core(s)

        def body(k, carry):
            zo, r = origin(s, k // 16), k % 16
            h = (r * 64 + T - STARTS[1]) // T
            rows = pl.ds(pl.multiple_of(r * 64 - h * STARTS[1], 64), 64)
            gain_rows = pl.ds(pl.multiple_of(PARTS[0] + h * (PARTS[1] - PARTS[0]), 16), GAIN_ROWS)
            to = pl.ds(pl.multiple_of(r * 64, 64), 64)
            squares = None
            for b in range(4):
                jj = zo * 4 + b
                block = xg[h, jj, rows, :].astype(F32)
                gains = jnp.sum(xg[h, jj, gain_rows, :].astype(F32), axis=0, keepdims=True)
                xs[zo, to, b * F:(b + 1) * F] = (block * gains).astype(BF16)
                squares = block * block if squares is None else squares + block * block
            ssq[to, :] += squares
            return carry

        lax.fori_loop(0, 16 * n_origins(s), body, 0)

    def multiply(s):
        origins = [origin(s, k) for k in range(n_origins(s))]

        def body(h, carry):
            into = pl.ds(pl.multiple_of(8 + h * H, 8), H)
            rows = pl.ds(pl.multiple_of(h * H, H), H)
            left = jnp.concatenate([xs[zo, rows, :] for zo in origins], axis=1)
            right = jnp.concatenate(
                [
                    jnp.concatenate([wg[zo, half, q] for zo in origins for half in range(2)], axis=0)
                    for q in range(3)
                ],
                axis=1,
            )
            product = jnp.dot(left, right, preferred_element_type=F32)
            for q in range(3):
                ext[q, into, :] += product[:, q * F:(q + 1) * F]
            return carry

        lax.fori_loop(0, 2, body, 0)

    def o_send(ii, half, dev):
        send("o", wo.at[ii, half], wo.at[ii, half], wor.at[ii, half, 0], dev)

    def o_wait(ii, half):
        arrived(wo.at[ii, half], wor.at[ii, half, 0])

    far, pfar = (i + 4) % NI, (pair + 4) % NI
    others = [(ii + k) % NI for ii in (i, pair) for k in (2, 6, 4)]

    def pass_on(wait, forward, block):
        below, above = (block + NI - 2) % NI, (block + 2) % NI
        for half in (0, 1):
            wait(below, half)
            if half == 0:
                forward(below, 0, dev_xu)
            wait(above, half)
            if half == 1:
                forward(above, 1, dev_xd)

    x_step(1)
    for half in range(2):
        w_wait(pair, half)
        for dev in (dev_xu, dev_xd):
            w_send(pair, half, dev)
    pass_on(w_wait, w_send, i)
    prepare(0)
    for yy, cc in ((yl, 1 - c), (1 - yl, c), (1 - yl, 1 - c)):
        rows = pl.ds(pl.multiple_of(cc * F, F), F)
        arrived(wo.at[i, yy, rows, :], wor.at[i, yy, cc])
    for half in range(2):
        o_send(i, half, dev_yh)
    x_step(2)
    x_late(1)
    pass_on(w_wait, w_send, pair)
    prepare(1)
    x_step(3)
    x_late(2)
    prepare(2)
    for ii in (far, pfar):
        for half in range(2):
            w_wait(ii, half)
    for half in range(2):
        for dev in (dev_xu, dev_xd):
            o_send(i, half, dev)
    for half in range(2):
        o_wait(pair, half)
        for dev in (dev_xu, dev_xd):
            o_send(pair, half, dev)
    multiply(0)
    x_late(3)
    x_step(4, ("own0",))
    multiply(1)
    x_step(4, ("own1", "par1"))
    multiply(2)
    prepare(3)
    x_late(4)
    pass_on(o_wait, o_send, i)
    multiply(3)
    prepare(4)
    multiply(4)

    def normalise(r, carry):
        rows = pl.ds(pl.multiple_of(r * 128, 128), 128)
        into = pl.ds(pl.multiple_of(8 + r * 128, 8), 128)
        total = jnp.sum(ssq[rows, :], axis=1, keepdims=True)
        inverse = lax.rsqrt(total * (1.0 / D) + 1e-06)
        ext[:, into, :] = (ext[:, into, :] * inverse[None]).astype(BF16).astype(F32)
        return carry

    normalise(T // 128 - 1, 0)
    halo = transfer("halo", ext.at[:, pl.ds(T, 8)], ext.at[:, pl.ds(0, 8)], hr, ((i + 1) % NI, j))
    pl.when(i < NI - 1)(halo.start)
    lax.fori_loop(0, T // 128 - 1, normalise, 0)

    rate_t, resid_t = rate[...], resid[...]
    scale_t = jnp.sqrt(one_minus_exp_neg(2.0 * rate_t))
    weight_t = resid_t * scale_t
    lam_t = jnp.exp(-rate_t)

    def wide(table, n):
        return jnp.broadcast_to(table[n:n + 1, :], (CH, F))

    lam = [wide(lam_t, n) for n in range(ORDER)]
    tap = lambda t, q: jnp.broadcast_to(filt[t, q:q + 1, :], (CH, F))

    def chunk_rows(start, q):
        return ext[q, pl.ds(start, CH, stride=CL), :]

    kt, vt = [tap(t, 1) for t in range(3)], [tap(t, 2) for t in range(3)]

    def mix(k0, k1, k2, v0, v1, v2):
        keys = kt[0] * k0 + kt[1] * k1 + kt[2] * k2
        values = vt[0] * v0 + vt[1] * v1 + vt[2] * v2
        return (keys * values).astype(BF16).astype(F32)

    U = 6

    def first(it, carry):
        k1, k2, v1, v2 = carry[:4]
        state = list(carry[4:])
        for u in range(U):
            s = 2 + it * U + u
            k0, v0 = chunk_rows(8 + s, 1), chunk_rows(8 + s, 2)
            m = mix(k0, k1, k2, v0, v1, v2)
            mx[s] = m
            state = [lam[n] * state[n] + m for n in range(ORDER)]
            k1, k2, v1, v2 = k0, k1, v0, v1
        return (k1, k2, v1, v2, *state)

    zero = jnp.zeros((CH, F), F32)
    state = lax.fori_loop(
        0, (CL - 2) // U, first,
        (chunk_rows(9, 1), chunk_rows(8, 1), chunk_rows(9, 2), chunk_rows(8, 2)) + (zero,) * ORDER,
    )[4:]

    @pl.when(i == 0)
    def _():
        ext[:, 6:8, :] = tail[...].astype(F32)

    @pl.when(i > 0)
    def _():
        arrived(ext.at[:, pl.ds(0, 8)], hr)

    heads = [mix(*(chunk_rows(8 + s - back, q) for q in (1, 2) for back in range(3))) for s in range(2)]
    mx[0], mx[1] = heads
    row8 = lax.broadcasted_iota(jnp.int32, (CH, F), 0)
    for n in range(ORDER):
        r = jnp.broadcast_to(rate_t[n:n + 1, :], (CH, F))
        total = state[n] + jnp.exp(-r * float(CL - 2)) * (lam[n] * heads[0] + heads[1])
        for shift in (1, 2, 4):
            moved = jnp.where(row8 >= shift, pltpu.roll(total, shift, axis=0), 0.0)
            total = total + jnp.exp(-r * float(CL * shift)) * moved
        ts[n] = total
        endb[n:n + 1, :] = total[CH - 1:CH, :]
    ends[i] = endb[...]
    for k in (3, 5, 4, 1, 7, 2, 6):
        send("ends", endb, ends.at[i], er.at[i], ((i + k) % NI, j))
    start_t = st_in[...] / scale_t
    pass_on(o_wait, o_send, pair)
    whole = jnp.exp(-rate_t * float(T))
    for k in range(1, NI):
        arrived(ends.at[(i + k) % NI], er.at[(i + k) % NI])
    now, mine = start_t, start_t
    for k in range(NI):
        mine = jnp.where(i == k, now, mine)
        now = whole * now + ends[k]
    st_out[...] = now * scale_t

    qt = [tap(t, 0) for t in range(3)]
    weight = [wide(weight_t, n) for n in range(ORDER)]
    direct = jnp.broadcast_to(skip[...], (CH, F))
    chunk_start = row8.astype(F32) * float(CL)
    entering = []
    for n in range(ORDER):
        r = jnp.broadcast_to(rate_t[n:n + 1, :], (CH, F))
        before = jnp.where(row8 >= 1, pltpu.roll(ts[n], 1, axis=0), 0.0)
        entering.append(before + jnp.exp(-r * chunk_start) * jnp.broadcast_to(mine[n:n + 1, :], (CH, F)))

    V = 4

    def second(it, carry):
        q1, q2 = carry[:2]
        state = list(carry[2:])
        for u in range(V):
            s = it * V + u
            q0 = chunk_rows(8 + s, 0)
            query = qt[0] * q0 + qt[1] * q1 + qt[2] * q2
            m = mx[s]
            state = [lam[n] * state[n] + m for n in range(ORDER)]
            terms = [weight[n] * state[n] for n in range(ORDER)] + [direct * m]
            while len(terms) > 1:
                terms = [a + b for a, b in zip(terms[::2], terms[1::2])] + terms[len(terms) & ~1:]
            gf[pl.ds(s, CH, stride=CL), :] = query * terms[0]
            q1, q2 = q0, q1
        return (q1, q2, *state)

    def g_send(p, yy, dev):
        send("g", gk.at[p, yy * 2 + c], gk.at[p, yy * 2 + c], gr.at[p, yy * 2 + c], dev)

    def g_wait(p, slot):
        arrived(gk.at[p, slot], gr.at[p, slot])

    carry = (chunk_rows(7, 0), chunk_rows(6, 0), *entering)
    for p in range(NP):
        carry = lax.fori_loop(p * PR // V, (p + 1) * PR // V, second, carry)
        for k in range(CH):
            start = k * CL + p * PR
            gk[p, yl * 2 + c, k * PR:(k + 1) * PR, :] = gf[start:start + PR, :].astype(BF16)
        g_send(p, yl, dev_y)
        g_send(p, yl, dev_c)
    for p in range(NP):
        g_wait(p, (1 - yl) * 2 + c)
        g_send(p, 1 - yl, dev_c)
        if p == 0:
            for ii in (far, pfar):
                for half in range(2):
                    o_wait(ii, half)

    def partial(p, first_to, second_to):
        left = jnp.concatenate([gk[p, slot] for slot in range(4)], axis=1)
        right = jnp.concatenate(
            [jnp.concatenate([wo[to, half] for half in range(2)], axis=0) for to in (first_to, second_to)], axis=1
        )
        product = jnp.dot(left, right, preferred_element_type=F32)
        pa[p, first_to] = product[:, 0:F]
        pa[p, second_to] = product[:, F:2 * F]

    steps = {(d, p): 4 if d == p % 2 else 3 for d in range(2) for p in range(NP)}

    def target(d, p, s):
        n = steps[d, p]
        return (z + n - s) % NZ if d == 0 else (z + NZ - n + s) % NZ

    def pass_sum(d, p, s):
        total = pa[p, target(d, p, s)]
        if s > 0:
            arrived(rb.at[d, p, s - 1], rr.at[d, p, s - 1])
            total = total + rb[d, p, s - 1].astype(F32)
        n = counts["sum"]
        sb[n] = total.astype(BF16)
        send("sum", sb.at[n], rb.at[d, p, s], rr.at[d, p, s], dev_up if d == 0 else dev_down)

    for p in range(NP):
        g_wait(p, yl * 2 + 1 - c)
        g_wait(p, (1 - yl) * 2 + 1 - c)
        partial(p, target(0, p, 0), target(1, p, 0))
        pass_sum(0, p, 0)
        pass_sum(1, p, 0)
    for s in range(1, 4):
        for p in range(NP):
            if s < 3:
                partial(p, target(0, p, s), target(1, p, s))
            else:
                partial(p, target(p % 2, p, 3), z)
            for d in range(2):
                if s < steps[d, p]:
                    pass_sum(d, p, s)
    for p in range(NP):
        total = pa[p, z]
        for d in range(2):
            last = steps[d, p] - 1
            arrived(rb.at[d, p, last], rr.at[d, p, last])
            total = total + rb[d, p, last].astype(F32)
        for k in range(CH):
            start = k * CL + p * PR
            rows = slice(start, start + PR)
            h = int(start >= STARTS[1])
            before = xg[h, j, start - STARTS[h]:start - STARTS[h] + PR, :]
            out[rows, :] = (total[k * PR:(k + 1) * PR, :] + before.astype(F32)).astype(BF16)

    for group, refs in (
        ("x0", xg.at[0, pl.ds(0, counts["x0"]), pl.ds(0, PARTS[0] + GAIN_ROWS), :]),
        ("x1", xg.at[1, pl.ds(0, counts["x1"]), pl.ds(0, PARTS[1] + GAIN_ROWS), :]),
        ("w", wg.at[pl.ds(0, counts["w"] // 2)]),
        ("o", wo.at[pl.ds(0, counts["o"] // 2)]),
        ("ws", ws.at[pl.ds(0, counts["ws"])]),
        ("ends", ends.at[pl.ds(0, counts["ends"])]),
        ("g", gk.at[:, pl.ds(0, counts["g"] // NP)]),
        ("sum", sb.at[pl.ds(0, counts["sum"])]),
    ):
        all_sent(group, refs)
    pl.when(i < NI - 1)(halo.wait_send)


def local(activations, norm_gain, w_in, tail_rows, short_filter, decay_rate, residue, skip_gain, state_in, w_out):
    vmem, anywhere = pl.BlockSpec(memory_space=pltpu.VMEM), pl.BlockSpec(memory_space=pl.ANY)
    dma = pltpu.SemaphoreType.DMA
    block_out, state_out = pl.pallas_call(
        block_kernel,
        out_shape=(jax.ShapeDtypeStruct((T, F), BF16), jax.ShapeDtypeStruct((ORDER, F), F32)),
        in_specs=[anywhere, vmem, anywhere, *[vmem] * 6, anywhere],
        out_specs=(vmem, vmem),
        scratch_shapes=[
            pltpu.VMEM((2, NJ, max(PARTS) + GAIN_ROWS, F), BF16),
            pltpu.VMEM((NZ, T, 4 * F), BF16),
            pltpu.VMEM((NI, 2, 3, 256, F), BF16),
            pltpu.VMEM((3, T + 8, F), F32),
            pltpu.VMEM((T, F), F32),
            pltpu.VMEM((CL, CH, F), F32),
            pltpu.VMEM((ORDER, CH, F), F32),
            pltpu.VMEM((ORDER, F), F32),
            pltpu.VMEM((NI, ORDER, F), F32),
            pltpu.VMEM((T, F), F32),
            pltpu.VMEM((NP, 4, PT, F), BF16),
            pltpu.VMEM((4, F, F), BF16),
            pltpu.VMEM((NI, 2, 2 * F, F), BF16),
            pltpu.VMEM((NP, NZ, PT, F), F32),
            pltpu.VMEM((7 * NP, PT, F), BF16),
            pltpu.VMEM((2, NP, 4, PT, F), BF16),
            dma((len(GROUPS),)),
            dma((8,)),
            dma((2, NJ)),
            dma((NI, 2)),
            dma,
            dma((NI,)),
            dma((NI, 2, 2)),
            dma((NP, 4)),
            dma((2, NP, 4)),
        ],
        compiler_params=pltpu.CompilerParams(
            collective_id=0, has_side_effects=True, vmem_limit_bytes=56 << 20
        ),
    )(
        activations, norm_gain.reshape(1, F), w_in.transpose(1, 0, 2), tail_rows.transpose(0, 2, 1), short_filter,
        decay_rate.T, residue.T, skip_gain.reshape(1, F), state_in.T, w_out,
    )
    return block_out, state_out.T


def solution(mesh):
    placed = (
        P("ctx", "mp"),
        P("mp"),
        P("ctx", None, "mp"),
        P(None, "mp", None),
        P(None, None, "mp"),
        P("mp", None),
        P("mp", None),
        P("mp"),
        P("mp", None),
        P("mp", "ctx"),
    )
    return jax.shard_map(
        local, mesh=mesh, in_specs=placed, out_specs=(P("ctx", "mp"), P("mp", None)), check_vma=False
    )
```
